512 devices in a mesh: prow: 16 (over x, y), pcol: 32 (over z, core).
Axes of the slice: x: 4, y: 4, z: 16, core: 2. Of those that a mesh axis runs over, the one named last changes fastest.
Arguments:
- adjoint_trail: float32 [2, 16, 256, 1, 32, 256], P(None, 'prow', None, None, 'pcol'), as said below
- factor_low: float32 [2, 16, 32, 8, 4, 256], P(None, 'prow', 'pcol'), may hold values from -0.0625 to 0.0625
- adjoint_low: float32 [2, 16, 32, 8, 4, 256], P(None, 'prow', 'pcol'), may hold values from -6 to 6
- factor_top: float32 [10, 256, 256], P(None, 'pcol'), as said below
- adjoint_top: float32 [10, 256, 256], P(None, 'pcol'), may hold values from -6 to 6
- diag_inverse: float32 [4, 256, 256], P(None, 'pcol'), as said below
Outputs:
- grad_low: float32 [2, 16, 32, 8, 4, 256], P(None, 'prow', 'pcol')
- grad_top: float32 [10, 256, 256], P(None, 'pcol')
The draws below stay inside these ranges and needn't reach their ends.
Inputs may be any that keep to these rules, and one draw needn't show every extreme that they name: adjoint_trail reshaped row-major to 8192 x 8192 is symmetric. The diagonal blocks factor_top[j (j + 1) / 2 + j] are lower triangular with a positive diagonal. diag_inverse[j] is the inverse of factor_top[j (j + 1) / 2 + j].
All inputs are finite; a program needn't handle non-finite values.
Results may differ from the reference program's by a relative error of at most 0.00024.
Values sent between devices are 32-bit elements; how exact they have to be, the bound alone decides.
A program may use at most 64 MiB of HBM per device.

```python
import math
import jax
import jax.numpy as jnp
from jax import lax

NB = 256
K = 4
M = 8192
NBLK = 10
MROW = 2
MCOL = 1
RSUB = 8
N_PROW = 16
N_PCOL = 32


def draw_adjoint_trail(key, part):
    first = jax.random.fold_in(key, 0)
    raw = jax.random.normal(first, (M, M), jnp.float32)
    symmetric = (raw + raw.T) * 0.7071
    return symmetric.reshape(MROW, N_PROW, NB, MCOL, N_PCOL, NB)


def diagonal_blocks(key):
    first, second = jax.random.split(jax.random.fold_in(key, 11))
    pivots = jnp.exp(jax.random.uniform(first, (K, NB), jnp.float32, math.log(0.7), math.log(1.4)))
    below = jax.random.normal(second, (K, NB, NB), jnp.float32) * (0.4 / math.sqrt(NB))
    row_ids = lax.broadcasted_iota(jnp.int32, (K, NB, NB), 1)
    col_ids = lax.broadcasted_iota(jnp.int32, (K, NB, NB), 2)
    strict = jnp.where(row_ids > col_ids, below, 0.0)
    return strict + jnp.where(row_ids == col_ids, pivots[:, :, None], 0.0)


def draw_factor_top(key, part):
    blocks = diagonal_blocks(key)
    noise = jax.random.normal(jax.random.fold_in(key, 12), (NBLK, NB, NB), jnp.float32) * (1.0 / math.sqrt(NB))
    for panel in range(K):
        noise = noise.at[panel * (panel + 1) // 2 + panel].set(blocks[panel])
    return noise


def invert_lower(block):
    identity = jnp.eye(NB, dtype=jnp.float32)
    return jax.scipy.linalg.solve_triangular(block, identity, lower=True)


def draw_diag_inverse(key, part):
    return jax.vmap(invert_lower)(diagonal_blocks(key))


def steps_of(own_key, dims, cuts, least, high):
    def one(axis_at, parts):
        draws = jax.random.uniform(jax.random.fold_in(jax.random.fold_in(own_key, 6), axis_at), (parts,), jnp.float32, least / len(cuts), high / len(cuts))
        return jnp.repeat(jnp.exp(draws), dims[axis_at] // parts).reshape((-1,) + (1,) * (len(dims) - axis_at - 1))

    loudness = one(*cuts[0])
    for cut in cuts[1:]:
        loudness = loudness * one(*cut)
    return loudness


def bell_draw(own_key, shape, deviation, most, shards=(), held_as=jnp.bfloat16):
    level = steps_of(own_key, shape, shards, -0.22, 0.18) if shards else 1.0
    values = jax.random.normal(own_key, shape, jnp.float32) * deviation * level
    return jnp.minimum(jnp.maximum(values, -most), most).astype(held_as)


def setup_inputs(seed: int = 0) -> dict:
    streams_of = jax.random.split(jax.random.key(seed), 7)
    return {
        "adjoint_trail": draw_adjoint_trail(jax.random.fold_in(streams_of[6], 71), 0),
        "factor_low": bell_draw(streams_of[1], (MROW, N_PROW, N_PCOL, RSUB, K, NB), M ** -0.5, 0.0625, ((1, 16), (2, 32)), jnp.float32),
        "adjoint_low": bell_draw(streams_of[2], (MROW, N_PROW, N_PCOL, RSUB, K, NB), 1.0, 6.0, ((1, 16), (2, 32)), jnp.float32),
        "factor_top": draw_factor_top(jax.random.fold_in(streams_of[6], 71), 0),
        "adjoint_top": bell_draw(streams_of[4], (NBLK, NB, NB), 1.0, 6.0, ((1, 32),), jnp.float32),
        "diag_inverse": draw_diag_inverse(jax.random.fold_in(streams_of[6], 71), 0),
    }


HIGHEST = lax.Precision.HIGHEST

def matmul(left, right):
    return jnp.dot(left.astype(jnp.float32), right.astype(jnp.float32), precision=HIGHEST, preferred_element_type=jnp.float32)

def half_lower(square):
    size = square.shape[0]
    row_ids = lax.broadcasted_iota(jnp.int32, (size, size), 0)
    col_ids = lax.broadcasted_iota(jnp.int32, (size, size), 1)
    return jnp.where(row_ids > col_ids, square, jnp.where(row_ids == col_ids, 0.5 * square, 0.0))

def assemble(top_blocks, low_part):
    span = K * NB
    upper = jnp.zeros((span, span), jnp.float32)
    for row_block in range(K):
        for col_block in range(row_block + 1):
            piece = top_blocks[row_block * (row_block + 1) // 2 + col_block]
            if row_block == col_block:
                piece = jnp.tril(piece)
            upper = upper.at[row_block * NB:(row_block + 1) * NB, col_block * NB:(col_block + 1) * NB].set(piece)
    return jnp.concatenate([upper, low_part.reshape(M, span)], axis=0)

def reference(adjoint_trail, factor_low, adjoint_low, factor_top, adjoint_top, diag_inverse):
    span = K * NB
    order = span + M
    factor = assemble(factor_top, factor_low)
    adjoint = assemble(adjoint_top, adjoint_low)
    collected = jnp.zeros((order, order), jnp.float32).at[span:, span:].set(adjoint_trail.reshape(M, M))
    gradients = [None] * K
    diagonals = [None] * K
    for panel in reversed(range(K)):
        low = panel * NB
        high = low + NB
        columns = factor[high:, low:high]
        diagonal = factor[low:high, low:high]
        residual = adjoint[high:, low:high] - 2.0 * matmul(collected[high:, high:], columns)
        gradient = matmul(residual, diag_inverse[panel])
        lower_adj = jnp.tril(adjoint[low:high, low:high] - matmul(gradient.T, columns))
        inner = half_lower(matmul(diagonal.T, lower_adj))
        spread = matmul(diag_inverse[panel].T, matmul(inner, diag_inverse[panel]))
        diag_grad = 0.5 * (spread + spread.T)
        collected = collected.at[high:, low:high].set(0.5 * gradient)
        collected = collected.at[low:high, high:].set(0.5 * gradient.T)
        collected = collected.at[low:high, low:high].set(diag_grad)
        gradients[panel] = gradient
        diagonals[panel] = diag_grad
    grad_low = jnp.stack([gradients[p][span - (p + 1) * NB:] for p in range(K)], 1).reshape(factor_low.shape)
    blocks = []
    for row_block in range(K):
        for col_block in range(row_block + 1):
            if row_block == col_block:
                blocks.append(diagonals[col_block])
            else:
                offset = (row_block - col_block - 1) * NB
                blocks.append(gradients[col_block][offset:offset + NB])
    grad_top = jnp.stack(blocks)
    return (grad_low, grad_top)
```

```python
import jax
import jax.numpy as jnp
from jax import lax
from jax.experimental import pallas as pl
from jax.experimental.pallas import tpu as pltpu
from jax.sharding import PartitionSpec as P

NB = 256
K = 4
NBLK = 10
NTOP = NBLK + K
PROWS = 16
PCOLS = 32
CHIPS = 16

HIGHEST = lax.Precision.HIGHEST
MESH = pl.DeviceIdType.MESH
F32 = jnp.float32


def matmul(left, right):
    return jnp.dot(left, right, precision=HIGHEST, preferred_element_type=F32)


def inner_product(left, right):
    return lax.dot_general(
        left, right, (((0,), (0,)), ((), ())), precision=HIGHEST, preferred_element_type=F32
    )


def block_slot(row_block, col_block):
    return row_block * (row_block + 1) // 2 + col_block


def loop(low, high, body):
    lax.fori_loop(low, high, lambda i, carry: (body(i), carry)[1], 0)


def remote(src, dst, send, recv, row, col):
    return pltpu.make_async_remote_copy(
        src_ref=src, dst_ref=dst, send_sem=send, recv_sem=recv, device_id=(row, col), device_id_type=MESH
    )


class Spread:
    def __init__(self, buf, count, sems, place):
        self.buf, self.count, self.place = buf, count, place
        self.line_send, self.line_recv, self.flat_send, self.flat_recv, self.twin_send, self.twin_recv = sems

    def line_copy(self, step, origin):
        p, z, c = self.place
        tile = self.buf.at[p, origin, c]
        peer = lax.rem(z + step, CHIPS) * 2 + c
        return remote(tile, tile, self.line_send.at[step], self.line_recv.at[origin], p, peer)

    def flat_copy(self, step, block):
        p, z, c = self.place
        half = self.buf.at[block, :, c]
        return remote(
            half, half, self.flat_send.at[step], self.flat_recv.at[block], lax.rem(p + step, PROWS), z * 2 + c
        )

    def twin_copy(self, block, core):
        p, z, c = self.place
        half = self.buf.at[block, :, core]
        return remote(half, half, self.twin_send.at[block], self.twin_recv.at[block], p, z * 2 + 1 - c)

    def start_line(self):
        p, z, c = self.place

        @pl.when(p < self.count)
        def _():
            loop(1, CHIPS, lambda step: self.line_copy(step, z).start())

    def start_flat(self):
        p, z, c = self.place

        @pl.when(p < self.count)
        def _():
            loop(1, CHIPS, lambda step: self.line_copy(step, lax.rem(z + step, CHIPS)).wait_recv())
            loop(1, PROWS, lambda step: self.flat_copy(step, p).start())
            self.twin_copy(p, c).start()

    def forward(self):
        p, z, c = self.place

        def body(block):
            @pl.when(block != p)
            def _():
                self.flat_copy(1, block).wait_recv()
                self.twin_copy(block, c).start()

        loop(0, self.count, body)

    def finish(self):
        p, z, c = self.place
        loop(0, self.count, lambda block: self.twin_copy(block, 1 - c).wait_recv())

    def drain(self):
        p, z, c = self.place

        @pl.when(p < self.count)
        def _():
            loop(1, CHIPS, lambda step: self.line_copy(step, z).wait_send())
            loop(1, PROWS, lambda step: self.flat_copy(step, p).wait_send())

        loop(0, self.count, lambda block: self.twin_copy(block, c).wait_send())


def spread_sems(count):
    dma = pltpu.SemaphoreType.DMA
    return [dma((CHIPS,)), dma((CHIPS,)), dma((PROWS,)), dma((count,)), dma((count,)), dma((count,))]


def exchange_kernel(
    trail, factor, adjoint, top_factor, top_adjoint, inverse, low_out, known_out, open_out,
    gathered, partial, pieces, moved, solved, slices, corner, tiles, columns, sums, terms, home,
    ring_send, ring_recv, twin_send, twin_recv, moved_send, moved_recv, sum_send, sum_recv,
    home_send, home_recv, slice_send, slice_recv, tile_send, tile_recv, term_send, term_recv, *spreads
):
    p, q = lax.axis_index("prow"), lax.axis_index("pcol")
    z, c = q // 2, lax.rem(q, 2)
    place = (p, z, c)
    known = Spread(known_out, NTOP, spreads[:6], place)
    opened = Spread(open_out, NBLK, spreads[6:], place)

    def ring_copy(way, step):
        ahead = way == 0
        origin = lax.rem(z + CHIPS - step if ahead else z + step, CHIPS)
        peer = lax.rem(z + 1 if ahead else z + CHIPS - 1, CHIPS)
        part = gathered.at[:, origin * 2 + c]
        return part, peer * 2 + c, origin

    def ring_start(way, step):
        part, peer, _ = ring_copy(way, step)
        remote(part, part, ring_send.at[way, step], ring_recv.at[way, step], p, peer).start()

    def ring_wait(way, step):
        part, peer, origin = ring_copy(way, step)
        remote(part, part, ring_send.at[way, step - 1], ring_recv.at[way, step - 1], p, peer).wait_recv()
        return origin

    def ring_drain(way, step):
        part, peer, _ = ring_copy(way, step)
        remote(part, part, ring_send.at[way, step], ring_recv.at[way, step], p, peer).wait_send()

    def twin_copy(origin, core):
        part = gathered.at[:, origin * 2 + core]
        return remote(part, part, twin_send.at[origin], twin_recv.at[origin], p, z * 2 + 1 - c)

    gathered[:, pl.ds(q, 1)] = factor[...][:, None]
    ring_start(0, 0)
    ring_start(1, 0)
    twin_copy(z, c).start()

    @pl.when(p < NBLK)
    def _():
        known_out[pl.ds(p, 1), pl.ds(z, 1), pl.ds(c, 1)] = top_factor[pl.ds(lax.rem(p, NBLK), 1)][:, None, None]

    @pl.when((p >= NBLK) & (p < NTOP))
    def _():
        known_out[pl.ds(p, 1), pl.ds(z, 1), pl.ds(c, 1)] = inverse[pl.ds(lax.rem(p + 2, K), 1)][:, None, None]

    known.start_line()

    home_row, home_half = lax.rem(q, PROWS), q // PROWS

    def here_or_there(src, dst, send, recv, row, col, act):
        own = (row == p) & (col == q)

        @pl.when(own)
        def _():
            act(pltpu.make_async_copy(src, dst, recv), True)

        @pl.when(jnp.logical_not(own))
        def _():
            act(remote(src, dst, send, recv, row, col), False)

    def move_out(half, act):
        here_or_there(
            adjoint.at[half], moved.at[c], moved_send.at[half], moved_recv.at[c], z, half * PROWS + p, act
        )

    def start(copy, local):
        copy.start()

    def sent(copy, local):
        if not local:
            copy.wait_send()

    def arrived(copy, local):
        copy.wait() if local else copy.wait_recv()

    for half in range(2):
        move_out(half, start)

    def ring_step(step):
        origin = ring_wait(0, step)

        @pl.when(step < CHIPS // 2)
        def _():
            ring_start(0, step)

        twin_copy(origin, c).start()

        @pl.when(step < CHIPS // 2)
        def _():
            other = ring_wait(1, step)

            @pl.when(step < CHIPS // 2 - 1)
            def _():
                ring_start(1, step)

            twin_copy(other, c).start()

    loop(1, 5, ring_step)
    known.start_flat()
    loop(5, CHIPS // 2 + 1, ring_step)
    loop(0, CHIPS, lambda origin: twin_copy(origin, 1 - c).wait_recv())

    everything = gathered[...].reshape(2, NB, K * NB)
    image = inner_product(trail[0], everything[0]) + inner_product(trail[1], everything[1])
    partial[...] = image.reshape(PROWS, 16, K * NB)

    def sum_copy(step, source):
        target = lax.rem(p + step, PROWS)
        return remote(partial.at[target], pieces.at[source], sum_send.at[step], sum_recv.at[source], target, q)

    loop(1, PROWS, lambda step: sum_copy(step, p).start())
    pieces[pl.ds(p, 1)] = partial[pl.ds(p, 1)]

    known.forward()
    known.finish()
    for half in range(2):
        here_or_there(
            adjoint.at[0], moved.at[half], moved_send.at[0], moved_recv.at[half], home_row, 2 * p + half, arrived
        )

    loop(1, PROWS, lambda step: sum_copy(step, lax.rem(p + step, PROWS)).wait_recv())
    total = pieces[0]
    for source in range(1, PROWS):
        total = total + pieces[source]
    residual = moved[...].reshape(16, K * NB) - 2.0 * total

    def block(slot):
        return known_out[slot].reshape(NB, NB)

    parts = [residual[:, j * NB : (j + 1) * NB] for j in range(K)]
    for j in reversed(range(K)):
        parts[j] = matmul(parts[j], block(NBLK + j))
        for earlier in range(j):
            parts[earlier] = parts[earlier] - matmul(parts[j], block(block_slot(j, earlier)))
        solved[:, :, j * NB : (j + 1) * NB] = parts[j].reshape(2, 8, NB)
        for side in range(2):
            slices[2 * j + side] = parts[j][:, side * 128 : (side + 1) * 128]

    base, spot = (p // 8) * 8, lax.rem(p, 8)

    def slice_copy(step, source):
        target = lax.rem(spot + step, 8)
        return remote(slices.at[target], corner.at[source], slice_send.at[step], slice_recv.at[source], base + target, q)

    loop(1, 8, lambda step: slice_copy(step, spot).start())
    corner[pl.ds(spot, 1)] = slices[pl.ds(spot, 1)]

    def home_out(half, act):
        here_or_there(
            solved.at[half], home.at[home_half], home_send.at[half], home_recv.at[home_half],
            home_row, 2 * p + half, act,
        )

    for half in range(2):
        home_out(half, start)
    loop(1, 8, lambda step: slice_copy(step, lax.rem(spot + step, 8)).wait_recv())
    tiles[...] = corner[...].reshape(128, 128).T.reshape(16, 8, 128)

    panel, upper = spot // 2, lax.rem(spot, 2)
    quarter = home_half * 2 + p // 8

    def tile_out(k, act):
        here_or_there(
            tiles.at[k], columns.at[panel, quarter], tile_send.at[k], tile_recv.at[panel, quarter],
            home_row, upper * 16 + k, act,
        )

    loop(0, 16, lambda k: tile_out(k, start))

    def tile_in(index):
        j, part = index // 4, lax.rem(index, 4)
        source_row = lax.rem(part, 2) * 8 + 2 * j + home_half
        source_col = (part // 2) * PROWS + p
        here_or_there(
            tiles.at[0], columns.at[j, part], tile_send.at[0], tile_recv.at[j, part], source_row, source_col, arrived
        )

    loop(0, 16, tile_in)
    wide = jnp.concatenate([columns[:, part].reshape(32, 128) for part in range(4)], axis=1)
    gram = matmul(wide, gathered[...].reshape(2 * NB, K * NB))
    for j in range(K):
        for i in range(j + 1):
            terms[block_slot(j, i)] = gram[j * 8 : (j + 1) * 8, i * NB : (i + 1) * NB]

    def term_copy(target, source):
        return remote(terms.at[target], sums.at[source], term_send.at[target], term_recv.at[source], target, q)

    def each_term(act):
        def body(target):
            @pl.when(target != p)
            def _():
                act(term_copy(target, p))

        loop(0, NBLK, body)

    each_term(lambda copy: copy.start())

    @pl.when(p < NBLK)
    def _():
        own = lax.rem(p, NBLK)
        sums[pl.ds(p, 1)] = terms[pl.ds(own, 1)]

        def body(step):
            source = lax.rem(p + step, PROWS)
            term_copy(own, source).wait_recv()

        loop(1, PROWS, body)
        whole = sums[0]
        for source in range(1, PROWS):
            whole = whole + sums[source]
        open_out[pl.ds(p, 1), pl.ds(z, 1), pl.ds(c, 1)] = (top_adjoint[own] - whole)[None, None, None]

    opened.start_line()
    opened.start_flat()
    for half in range(2):
        here_or_there(
            solved.at[0], home.at[half], home_send.at[0], home_recv.at[half], z, half * PROWS + p, arrived
        )
    low_out[...] = home[...]
    opened.forward()
    opened.finish()

    for way in range(2):
        loop(0, CHIPS // 2 - way, lambda step: ring_drain(way, step))
    loop(0, CHIPS, lambda origin: twin_copy(origin, c).wait_send())
    for half in range(2):
        move_out(half, sent)
        home_out(half, sent)
    loop(1, PROWS, lambda step: sum_copy(step, p).wait_send())
    loop(1, 8, lambda step: slice_copy(step, spot).wait_send())
    loop(0, 16, lambda k: tile_out(k, sent))
    each_term(lambda copy: copy.wait_send())
    known.drain()
    opened.drain()


def half_lower(square):
    row_ids = lax.broadcasted_iota(jnp.int32, (NB, NB), 0)
    col_ids = lax.broadcasted_iota(jnp.int32, (NB, NB), 1)
    return jnp.where(row_ids > col_ids, square, jnp.where(row_ids == col_ids, 0.5 * square, 0.0))


def lower(square):
    row_ids = lax.broadcasted_iota(jnp.int32, (NB, NB), 0)
    col_ids = lax.broadcasted_iota(jnp.int32, (NB, NB), 1)
    return jnp.where(row_ids >= col_ids, square, 0.0)


def top_kernel(known, opened, out, full):
    def factor(r, j):
        return known[block_slot(r, j)].reshape(NB, NB)

    def inverse(j):
        return known[NBLK + j].reshape(NB, NB)

    def grad(r, j):
        return full[block_slot(r, j)]

    for j in reversed(range(K)):
        for r in range(j + 1, K):
            rest = opened[block_slot(r, j)].reshape(NB, NB) - 2.0 * matmul(grad(r, r), factor(r, j))
            for middle in range(j + 1, r):
                rest = rest - matmul(grad(r, middle), factor(middle, j))
            for beyond in range(r + 1, K):
                rest = rest - inner_product(grad(beyond, r), factor(beyond, j))
            full[block_slot(r, j)] = matmul(rest, inverse(j))
        adj = opened[block_slot(j, j)].reshape(NB, NB)
        for r in range(j + 1, K):
            adj = adj - inner_product(grad(r, j), factor(r, j))
        inner = half_lower(inner_product(lower(factor(j, j)), lower(adj)))
        spread = inner_product(inverse(j), matmul(inner, inverse(j)))
        full[block_slot(j, j)] = 0.5 * (spread + spread.T)
    rows = pl.ds(pl.multiple_of(lax.axis_index("pcol") * 8, 8), 8)
    out[...] = full[:, rows, :]


def per_device(adjoint_trail, factor_low, adjoint_low, factor_top, adjoint_top, diag_inverse):
    dma = pltpu.SemaphoreType.DMA
    vmem = pl.BlockSpec(memory_space=pltpu.VMEM)
    wide = K * NB
    low_grad, known, opened = pl.pallas_call(
        exchange_kernel,
        out_shape=[
            jax.ShapeDtypeStruct((2, 8, wide), F32),
            jax.ShapeDtypeStruct((NTOP, CHIPS, 2, 8, NB), F32),
            jax.ShapeDtypeStruct((NBLK, CHIPS, 2, 8, NB), F32),
        ],
        in_specs=[vmem] * 6,
        out_specs=[vmem] * 3,
        scratch_shapes=[
            pltpu.VMEM((2, PCOLS, 8, wide), F32),
            pltpu.VMEM((PROWS, 16, wide), F32),
            pltpu.VMEM((PROWS, 16, wide), F32),
            pltpu.VMEM((2, 8, wide), F32),
            pltpu.VMEM((2, 8, wide), F32),
            pltpu.VMEM((8, 16, 128), F32),
            pltpu.VMEM((8, 16, 128), F32),
            pltpu.VMEM((16, 8, 128), F32),
            pltpu.VMEM((4, 4, 8, 128), F32),
            pltpu.VMEM((PROWS, 8, NB), F32),
            pltpu.VMEM((NBLK, 8, NB), F32),
            pltpu.VMEM((2, 8, wide), F32),
            dma((2, 8)), dma((2, 8)), dma((CHIPS,)), dma((CHIPS,)), dma((2,)), dma((2,)),
            dma((PROWS,)), dma((PROWS,)), dma((2,)), dma((2,)), dma((8,)), dma((8,)),
            dma((16,)), dma((4, 4)), dma((NBLK,)), dma((PROWS,)),
            *spread_sems(NTOP),
            *spread_sems(NBLK),
        ],
        compiler_params=pltpu.CompilerParams(has_side_effects=True, vmem_limit_bytes=40 * 1024 * 1024),
        name="exchange",
    )(
        adjoint_trail.reshape(2, NB, NB),
        factor_low.reshape(2, 8, wide),
        adjoint_low.reshape(2, 8, wide),
        factor_top,
        adjoint_top,
        diag_inverse,
    )
    grad_top = pl.pallas_call(
        top_kernel,
        out_shape=jax.ShapeDtypeStruct((NBLK, 8, NB), F32),
        in_specs=[vmem] * 2,
        out_specs=vmem,
        scratch_shapes=[pltpu.VMEM((NBLK, NB, NB), F32)],
        compiler_params=pltpu.CompilerParams(vmem_limit_bytes=40 * 1024 * 1024),
        name="top",
    )(known, opened)
    return low_grad.reshape(factor_low.shape), grad_top


def solution(mesh):
    in_specs = (
        P(None, "prow", None, None, "pcol", None),
        P(None, "prow", "pcol", None, None, None),
        P(None, "prow", "pcol", None, None, None),
        P(None, "pcol", None),
        P(None, "pcol", None),
        P(None, "pcol", None),
    )
    out_specs = (P(None, "prow", "pcol", None, None, None), P(None, "pcol", None))
    return jax.shard_map(
        per_device, mesh=mesh, in_specs=in_specs, out_specs=out_specs, check_vma=False
    )
```

```python
import jax
import jax.numpy as jnp
from jax import lax
from jax.experimental import pallas as pl
from jax.experimental.pallas import tpu as pltpu
from jax.sharding import PartitionSpec as P

NB = 256
K = 4
NBLK = 10
NTOP = NBLK + K
PROWS = 16
PCOLS = 32
CHIPS = 16
SIDE = 4

HIGHEST = lax.Precision.HIGHEST
MESH = pl.DeviceIdType.MESH
F32 = jnp.float32


def matmul(left, right):
    return jnp.dot(left, right, precision=HIGHEST, preferred_element_type=F32)


def inner_product(left, right):
    return lax.dot_general(
        left, right, (((0,), (0,)), ((), ())), precision=HIGHEST, preferred_element_type=F32
    )


def block_slot(row_block, col_block):
    return row_block * (row_block + 1) // 2 + col_block


def loop(low, high, body):
    lax.fori_loop(low, high, lambda i, carry: (body(i), carry)[1], 0)


def remote(src, dst, send, recv, row, col):
    return pltpu.make_async_remote_copy(
        src_ref=src, dst_ref=dst, send_sem=send, recv_sem=recv, device_id=(row, col), device_id_type=MESH
    )


class Spread:
    def __init__(self, buf, count, sems, place):
        self.buf, self.count, self.place = buf, count, place
        self.line_send, self.line_recv, self.near_send, self.far_send, self.flat_recv, self.twin_send, self.twin_recv = sems

    def line_copy(self, step, origin):
        p, z, c = self.place
        tile = self.buf.at[p, origin, c]
        peer = lax.rem(z + step, CHIPS) * 2 + c
        return remote(tile, tile, self.line_send.at[step], self.line_recv.at[origin], p, peer)

    def peers(self, step):
        p, z, c = self.place
        x, y = p // SIDE, lax.rem(p, SIDE)
        along_x = lax.rem(x + step, SIDE) * SIDE + y
        along_y = x * SIDE + lax.rem(y + step, SIDE)
        return along_x * (1 - c) + along_y * c, along_y * (1 - c) + along_x * c

    def near_copy(self, step):
        p, z, c = self.place
        half = self.buf.at[p, :, c]
        return remote(half, half, self.near_send.at[step], self.flat_recv.at[p], self.peers(step)[0], z * 2 + c)

    def far_copy(self, block, origin, step):
        p, z, c = self.place
        half = self.buf.at[block, :, c]
        return remote(
            half, half, self.far_send.at[origin, step], self.flat_recv.at[block], self.peers(step)[1], z * 2 + c
        )

    def twin_copy(self, block, core):
        p, z, c = self.place
        half = self.buf.at[block, :, core]
        return remote(half, half, self.twin_send.at[block], self.twin_recv.at[block], p, z * 2 + 1 - c)

    def start_line(self):
        p, z, c = self.place

        @pl.when(p < self.count)
        def _():
            loop(1, CHIPS, lambda step: self.line_copy(step, z).start())

    def start_flat(self):
        p, z, c = self.place

        @pl.when(p < self.count)
        def _():
            loop(1, CHIPS, lambda step: self.line_copy(step, lax.rem(z + step, CHIPS)).wait_recv())

            def body(step):
                self.near_copy(step).start()
                self.far_copy(p, 0, step).start()

            loop(1, SIDE, body)
            self.twin_copy(p, c).start()

    def relay(self):
        def body(origin):
            block = self.peers(origin)[0]

            @pl.when(block < self.count)
            def _():
                self.far_copy(block, origin, 1).wait_recv()
                loop(1, SIDE, lambda step: self.far_copy(block, origin, step).start())

        loop(1, SIDE, body)

    def share(self, block):
        p, z, c = self.place
        x, y = p // SIDE, lax.rem(p, SIDE)
        straight = (block // SIDE) * (1 - c) + lax.rem(block, SIDE) * c
        mine = x * (1 - c) + y * c
        cross = lax.rem(block, SIDE) * (1 - c) + (block // SIDE) * c
        level = y * (1 - c) + x * c

        @pl.when(block != p)
        def _():
            @pl.when((straight == mine) | (cross != level))
            def _():
                self.far_copy(block, 0, 1).wait_recv()

            self.twin_copy(block, c).start()

    def finish(self, block):
        p, z, c = self.place
        self.twin_copy(block, 1 - c).wait_recv()

    def drain(self):
        p, z, c = self.place

        @pl.when(p < self.count)
        def _():
            loop(1, CHIPS, lambda step: self.line_copy(step, z).wait_send())

            def body(step):
                self.near_copy(step).wait_send()
                self.far_copy(p, 0, step).wait_send()

            loop(1, SIDE, body)

        def relayed(origin):
            block = self.peers(origin)[0]

            @pl.when(block < self.count)
            def _():
                loop(1, SIDE, lambda step: self.far_copy(block, origin, step).wait_send())

        loop(1, SIDE, relayed)
        loop(0, self.count, lambda block: self.twin_copy(block, c).wait_send())


def spread_sems(count):
    dma = pltpu.SemaphoreType.DMA
    return [
        dma((CHIPS,)), dma((CHIPS,)), dma((SIDE,)), dma((SIDE, SIDE)), dma((PROWS,)), dma((count,)), dma((count,))
    ]


def exchange_kernel(
    trail, factor, adjoint, top_factor, top_adjoint, inverse, low_out, top_out,
    known_out, open_out, full, gathered, partial, pieces, moved, solved, slices, corner, tiles, columns, sums, terms, home,
    ring_send, ring_recv, twin_send, twin_recv, moved_send, moved_recv, sum_send, sum_recv,
    home_send, home_recv, slice_send, slice_recv, tile_send, tile_recv, term_send, term_recv, *spreads
):
    p, q = lax.axis_index("prow"), lax.axis_index("pcol")
    z, c = q // 2, lax.rem(q, 2)
    place = (p, z, c)
    known = Spread(known_out, NTOP, spreads[:7], place)
    opened = Spread(open_out, NBLK, spreads[7:], place)

    def ring_copy(way, half, step, slot):
        ahead = way == 0
        origin = lax.rem(z + CHIPS - step if ahead else z + step, CHIPS)
        peer = lax.rem(z + 1 if ahead else z + CHIPS - 1, CHIPS)
        part = gathered.at[half, origin * 2 + c]
        return remote(part, part, ring_send.at[way, half, slot], ring_recv.at[way, half, slot], p, peer * 2 + c)

    def ring_start(way, half, step):
        ring_copy(way, half, step, step).start()

    def ring_wait(way, half, step):
        ring_copy(way, half, step, step - 1).wait_recv()

    def twin_copy(origin, core):
        part = gathered.at[:, origin * 2 + core]
        return remote(part, part, twin_send.at[origin], twin_recv.at[origin], p, z * 2 + 1 - c)

    gathered[:, pl.ds(q, 1)] = factor[...][:, None]
    for half in range(2):
        for way in range(2):
            ring_start(way, half, 0)
    twin_copy(z, c).start()

    @pl.when(p < NBLK)
    def _():
        known_out[pl.ds(p, 1), pl.ds(z, 1), pl.ds(c, 1)] = top_factor[pl.ds(lax.rem(p, NBLK), 1)][:, None, None]

    @pl.when((p >= NBLK) & (p < NTOP))
    def _():
        known_out[pl.ds(p, 1), pl.ds(z, 1), pl.ds(c, 1)] = inverse[pl.ds(lax.rem(p + 2, K), 1)][:, None, None]

    known.start_line()

    home_row, home_half = lax.rem(q, PROWS), q // PROWS

    def here_or_there(src, dst, send, recv, row, col, act):
        own = (row == p) & (col == q)

        @pl.when(own)
        def _():
            act(pltpu.make_async_copy(src, dst, recv), True)

        @pl.when(jnp.logical_not(own))
        def _():
            act(remote(src, dst, send, recv, row, col), False)

    def move_out(half, act):
        here_or_there(
            adjoint.at[half], moved.at[c], moved_send.at[half], moved_recv.at[c], z, half * PROWS + p, act
        )

    def start(copy, local):
        copy.start()

    def sent(copy, local):
        if not local:
            copy.wait_send()

    def arrived(copy, local):
        copy.wait() if local else copy.wait_recv()

    for half in range(2):
        move_out(half, start)

    def ring_step(step):
        for half in range(2):
            ring_wait(0, half, step)

            @pl.when(step < CHIPS // 2)
            def _():
                ring_start(0, half, step)
                ring_wait(1, half, step)

            @pl.when(step < CHIPS // 2 - 1)
            def _():
                ring_start(1, half, step)

        twin_copy(lax.rem(z + CHIPS - step, CHIPS), c).start()

        @pl.when(step < CHIPS // 2)
        def _():
            twin_copy(lax.rem(z + step, CHIPS), c).start()

    loop(1, 4, ring_step)
    known.start_flat()
    loop(4, 7, ring_step)
    known.relay()
    loop(7, CHIPS // 2 + 1, ring_step)
    loop(0, CHIPS, lambda origin: twin_copy(origin, 1 - c).wait_recv())

    everything = gathered[...].reshape(2, NB, K * NB)
    image = inner_product(trail[0], everything[0]) + inner_product(trail[1], everything[1])
    partial[...] = image.reshape(PROWS, 16, K * NB)

    def sum_copy(step, source):
        target = lax.rem(p + step, PROWS)
        return remote(partial.at[target], pieces.at[source], sum_send.at[step], sum_recv.at[source], target, q)

    loop(1, PROWS, lambda step: sum_copy(step, p).start())
    pieces[pl.ds(p, 1)] = partial[pl.ds(p, 1)]

    loop(0, NTOP, known.share)
    loop(0, NTOP, known.finish)
    for half in range(2):
        here_or_there(
            adjoint.at[0], moved.at[half], moved_send.at[0], moved_recv.at[half], home_row, 2 * p + half, arrived
        )

    loop(1, PROWS, lambda step: sum_copy(step, lax.rem(p + step, PROWS)).wait_recv())
    total = pieces[0]
    for source in range(1, PROWS):
        total = total + pieces[source]
    residual = moved[...].reshape(16, K * NB) - 2.0 * total

    def block(slot):
        return known_out[slot].reshape(NB, NB)

    parts = [residual[:, j * NB : (j + 1) * NB] for j in range(K)]
    for j in reversed(range(K)):
        parts[j] = matmul(parts[j], block(NBLK + j))
        for earlier in range(j):
            parts[earlier] = parts[earlier] - matmul(parts[j], block(block_slot(j, earlier)))
        solved[:, :, j * NB : (j + 1) * NB] = parts[j].reshape(2, 8, NB)
        for side in range(2):
            slices[2 * j + side] = parts[j][:, side * 128 : (side + 1) * 128]

    base, spot = (p // 8) * 8, lax.rem(p, 8)

    def slice_copy(step, source):
        target = lax.rem(spot + step, 8)
        return remote(slices.at[target], corner.at[source], slice_send.at[step], slice_recv.at[source], base + target, q)

    loop(1, 8, lambda step: slice_copy(step, spot).start())
    corner[pl.ds(spot, 1)] = slices[pl.ds(spot, 1)]

    def home_out(half, act):
        here_or_there(
            solved.at[half], home.at[home_half], home_send.at[half], home_recv.at[home_half],
            home_row, 2 * p + half, act,
        )

    for half in range(2):
        home_out(half, start)
    loop(1, 8, lambda step: slice_copy(step, lax.rem(spot + step, 8)).wait_recv())
    tiles[...] = corner[...].reshape(128, 128).T.reshape(16, 8, 128)

    panel, upper = spot // 2, lax.rem(spot, 2)
    quarter = home_half * 2 + p // 8

    def tile_out(k, act):
        here_or_there(
            tiles.at[k], columns.at[panel, quarter], tile_send.at[k], tile_recv.at[panel, quarter],
            home_row, upper * 16 + k, act,
        )

    loop(0, 16, lambda k: tile_out(k, start))

    def tile_in(index):
        j, part = index // 4, lax.rem(index, 4)
        source_row = lax.rem(part, 2) * 8 + 2 * j + home_half
        source_col = (part // 2) * PROWS + p
        here_or_there(
            tiles.at[0], columns.at[j, part], tile_send.at[0], tile_recv.at[j, part], source_row, source_col, arrived
        )

    loop(0, 16, tile_in)
    wide = jnp.concatenate([columns[:, part].reshape(32, 128) for part in range(4)], axis=1)
    gram = matmul(wide, gathered[...].reshape(2 * NB, K * NB))
    for j in range(K):
        for i in range(j + 1):
            terms[block_slot(j, i)] = gram[j * 8 : (j + 1) * 8, i * NB : (i + 1) * NB]

    def term_copy(target, source):
        return remote(terms.at[target], sums.at[source], term_send.at[target], term_recv.at[source], target, q)

    def each_term(act):
        def body(target):
            @pl.when(target != p)
            def _():
                act(term_copy(target, p))

        loop(0, NBLK, body)

    each_term(lambda copy: copy.start())

    @pl.when(p < NBLK)
    def _():
        own = lax.rem(p, NBLK)
        sums[pl.ds(p, 1)] = terms[pl.ds(own, 1)]

        def body(step):
            source = lax.rem(p + step, PROWS)
            term_copy(own, source).wait_recv()

        loop(1, PROWS, body)
        whole = sums[0]
        for source in range(1, PROWS):
            whole = whole + sums[source]
        open_out[pl.ds(p, 1), pl.ds(z, 1), pl.ds(c, 1)] = (top_adjoint[own] - whole)[None, None, None]

    opened.start_line()
    opened.start_flat()
    opened.relay()

    def share_column(j):
        for r in range(j, K):
            opened.share(block_slot(r, j))

    share_column(K - 1)
    share_column(K - 2)
    for j in reversed(range(K)):
        for r in range(j, K):
            opened.finish(block_slot(r, j))
        top_column(j, known_out, open_out, full)
        if j >= 2:
            share_column(j - 2)
    top_out[...] = full[:, pl.ds(pl.multiple_of(q * 8, 8), 8), :]
    for half in range(2):
        here_or_there(
            solved.at[0], home.at[half], home_send.at[0], home_recv.at[half], z, half * PROWS + p, arrived
        )
    low_out[...] = home[...]

    for half in range(2):
        for way in range(2):
            loop(0, CHIPS // 2 - way, lambda step: ring_copy(way, half, step, step).wait_send())
    loop(0, CHIPS, lambda origin: twin_copy(origin, c).wait_send())
    for half in range(2):
        move_out(half, sent)
        home_out(half, sent)
    loop(1, PROWS, lambda step: sum_copy(step, p).wait_send())
    loop(1, 8, lambda step: slice_copy(step, spot).wait_send())
    loop(0, 16, lambda k: tile_out(k, sent))
    each_term(lambda copy: copy.wait_send())
    known.drain()
    opened.drain()


def half_lower(square):
    row_ids = lax.broadcasted_iota(jnp.int32, (NB, NB), 0)
    col_ids = lax.broadcasted_iota(jnp.int32, (NB, NB), 1)
    return jnp.where(row_ids > col_ids, square, jnp.where(row_ids == col_ids, 0.5 * square, 0.0))


def lower(square):
    row_ids = lax.broadcasted_iota(jnp.int32, (NB, NB), 0)
    col_ids = lax.broadcasted_iota(jnp.int32, (NB, NB), 1)
    return jnp.where(row_ids >= col_ids, square, 0.0)


def top_column(j, known, opened, full):
    def factor(r, j):
        return known[block_slot(r, j)].reshape(NB, NB)

    def grad(r, j):
        return full[block_slot(r, j)]

    inverse = known[NBLK + j].reshape(NB, NB)
    for r in range(j + 1, K):
        rest = opened[block_slot(r, j)].reshape(NB, NB) - 2.0 * matmul(grad(r, r), factor(r, j))
        for middle in range(j + 1, r):
            rest = rest - matmul(grad(r, middle), factor(middle, j))
        for beyond in range(r + 1, K):
            rest = rest - inner_product(grad(beyond, r), factor(beyond, j))
        full[block_slot(r, j)] = matmul(rest, inverse)
    adj = opened[block_slot(j, j)].reshape(NB, NB)
    for r in range(j + 1, K):
        adj = adj - inner_product(grad(r, j), factor(r, j))
    inner = half_lower(inner_product(lower(factor(j, j)), lower(adj)))
    spread = inner_product(inverse, matmul(inner, inverse))
    full[block_slot(j, j)] = 0.5 * (spread + spread.T)


def per_device(adjoint_trail, factor_low, adjoint_low, factor_top, adjoint_top, diag_inverse):
    dma = pltpu.SemaphoreType.DMA
    vmem = pl.BlockSpec(memory_space=pltpu.VMEM)
    wide = K * NB
    low_grad, grad_top = pl.pallas_call(
        exchange_kernel,
        out_shape=[
            jax.ShapeDtypeStruct((2, 8, wide), F32),
            jax.ShapeDtypeStruct((NBLK, 8, NB), F32),
        ],
        in_specs=[vmem] * 6,
        out_specs=[vmem] * 2,
        scratch_shapes=[
            pltpu.VMEM((NTOP, CHIPS, 2, 8, NB), F32),
            pltpu.VMEM((NBLK, CHIPS, 2, 8, NB), F32),
            pltpu.VMEM((NBLK, NB, NB), F32),
            pltpu.VMEM((2, PCOLS, 8, wide), F32),
            pltpu.VMEM((PROWS, 16, wide), F32),
            pltpu.VMEM((PROWS, 16, wide), F32),
            pltpu.VMEM((2, 8, wide), F32),
            pltpu.VMEM((2, 8, wide), F32),
            pltpu.VMEM((8, 16, 128), F32),
            pltpu.VMEM((8, 16, 128), F32),
            pltpu.VMEM((16, 8, 128), F32),
            pltpu.VMEM((4, 4, 8, 128), F32),
            pltpu.VMEM((PROWS, 8, NB), F32),
            pltpu.VMEM((NBLK, 8, NB), F32),
            pltpu.VMEM((2, 8, wide), F32),
            dma((2, 2, 8)), dma((2, 2, 8)), dma((CHIPS,)), dma((CHIPS,)), dma((2,)), dma((2,)),
            dma((PROWS,)), dma((PROWS,)), dma((2,)), dma((2,)), dma((8,)), dma((8,)),
            dma((16,)), dma((4, 4)), dma((NBLK,)), dma((PROWS,)),
            *spread_sems(NTOP),
            *spread_sems(NBLK),
        ],
        compiler_params=pltpu.CompilerParams(has_side_effects=True, vmem_limit_bytes=40 * 1024 * 1024),
        name="exchange",
    )(
        adjoint_trail.reshape(2, NB, NB),
        factor_low.reshape(2, 8, wide),
        adjoint_low.reshape(2, 8, wide),
        factor_top,
        adjoint_top,
        diag_inverse,
    )
    return low_grad.reshape(factor_low.shape), grad_top


def solution(mesh):
    in_specs = (
        P(None, "prow", None, None, "pcol", None),
        P(None, "prow", "pcol", None, None, None),
        P(None, "prow", "pcol", None, None, None),
        P(None, "pcol", None),
        P(None, "pcol", None),
        P(None, "pcol", None),
    )
    out_specs = (P(None, "prow", "pcol", None, None, None), P(None, "pcol", None))
    return jax.shard_map(
        per_device, mesh=mesh, in_specs=in_specs, out_specs=out_specs, check_vma=False
    )
```

```python
import jax
import jax.numpy as jnp
from jax import lax
from jax.experimental import pallas as pl
from jax.experimental.pallas import tpu as pltpu
from jax.sharding import PartitionSpec as P

NB = 256
K = 4
NBLK = 10
NTOP = NBLK + K
PROWS = 16
PCOLS = 32
CHIPS = 16
SIDE = 4

HIGHEST = lax.Precision.HIGHEST
MESH = pl.DeviceIdType.MESH
F32 = jnp.float32


def matmul(left, right):
    return jnp.dot(left, right, precision=HIGHEST, preferred_element_type=F32)


def inner_product(left, right):
    return lax.dot_general(
        left, right, (((0,), (0,)), ((), ())), precision=HIGHEST, preferred_element_type=F32
    )


def block_slot(row_block, col_block):
    return row_block * (row_block + 1) // 2 + col_block


def loop(low, high, body):
    lax.fori_loop(low, high, lambda i, carry: (body(i), carry)[1], 0)


def remote(src, dst, send, recv, row, col):
    return pltpu.make_async_remote_copy(
        src_ref=src, dst_ref=dst, send_sem=send, recv_sem=recv, device_id=(row, col), device_id_type=MESH
    )


def far_first(index):
    rest = CHIPS - index
    odd = lax.rem(rest, 2)
    return (rest // 2 + 1) * odd + (CHIPS - rest // 2) * (1 - odd)


class Spread:
    def __init__(self, buf, count, sems, place):
        self.buf, self.count, self.place = buf, count, place
        self.line_send, self.line_recv, self.near_send, self.far_send, self.flat_recv, self.twin_send, self.twin_recv = sems

    def line_copy(self, step, origin):
        p, z, c = self.place
        tile = self.buf.at[p, origin, c]
        peer = lax.rem(z + step, CHIPS) * 2 + c
        return remote(tile, tile, self.line_send.at[step], self.line_recv.at[origin], p, peer)

    def peers(self, step):
        p, z, c = self.place
        x, y = p // SIDE, lax.rem(p, SIDE)
        along_x = lax.rem(x + step, SIDE) * SIDE + y
        along_y = x * SIDE + lax.rem(y + step, SIDE)
        return along_x * (1 - c) + along_y * c, along_y * (1 - c) + along_x * c

    def near_copy(self, step):
        p, z, c = self.place
        half = self.buf.at[p, :, c]
        return remote(half, half, self.near_send.at[step], self.flat_recv.at[p], self.peers(step)[0], z * 2 + c)

    def far_copy(self, block, origin, step):
        p, z, c = self.place
        half = self.buf.at[block, :, c]
        return remote(
            half, half, self.far_send.at[origin, step], self.flat_recv.at[block], self.peers(step)[1], z * 2 + c
        )

    def twin_copy(self, block, core):
        p, z, c = self.place
        half = self.buf.at[block, :, core]
        return remote(half, half, self.twin_send.at[block], self.twin_recv.at[block], p, z * 2 + 1 - c)

    def start_line(self):
        p, z, c = self.place

        @pl.when(p < self.count)
        def _():
            loop(1, CHIPS, lambda index: self.line_copy(far_first(index), z).start())

    def start_flat(self):
        p, z, c = self.place

        @pl.when(p < self.count)
        def _():
            loop(1, CHIPS, lambda step: self.line_copy(step, lax.rem(z + step, CHIPS)).wait_recv())

            def body(step):
                self.near_copy(step).start()
                self.far_copy(p, 0, step).start()

            loop(1, SIDE, body)
            self.twin_copy(p, c).start()

    def relay(self):
        def body(origin):
            block = self.peers(origin)[0]

            @pl.when(block < self.count)
            def _():
                self.far_copy(block, origin, 1).wait_recv()
                loop(1, SIDE, lambda step: self.far_copy(block, origin, step).start())

        loop(1, SIDE, body)

    def share(self, block):
        p, z, c = self.place
        x, y = p // SIDE, lax.rem(p, SIDE)
        straight = (block // SIDE) * (1 - c) + lax.rem(block, SIDE) * c
        mine = x * (1 - c) + y * c
        cross = lax.rem(block, SIDE) * (1 - c) + (block // SIDE) * c
        level = y * (1 - c) + x * c

        @pl.when(block != p)
        def _():
            @pl.when((straight == mine) | (cross != level))
            def _():
                self.far_copy(block, 0, 1).wait_recv()

            self.twin_copy(block, c).start()

    def finish(self, block):
        p, z, c = self.place
        self.twin_copy(block, 1 - c).wait_recv()

    def drain(self):
        p, z, c = self.place

        @pl.when(p < self.count)
        def _():
            loop(1, CHIPS, lambda step: self.line_copy(step, z).wait_send())

            def body(step):
                self.near_copy(step).wait_send()
                self.far_copy(p, 0, step).wait_send()

            loop(1, SIDE, body)

        def relayed(origin):
            block = self.peers(origin)[0]

            @pl.when(block < self.count)
            def _():
                loop(1, SIDE, lambda step: self.far_copy(block, origin, step).wait_send())

        loop(1, SIDE, relayed)
        loop(0, self.count, lambda block: self.twin_copy(block, c).wait_send())


def spread_sems(count):
    dma = pltpu.SemaphoreType.DMA
    return [
        dma((CHIPS,)), dma((CHIPS,)), dma((SIDE,)), dma((SIDE, SIDE)), dma((PROWS,)), dma((count,)), dma((count,))
    ]


def exchange_kernel(
    trail, factor_in, adjoint_in, factor_top_in, adjoint_top_in, inverse_in, low_out, top_out,
    factor, adjoint_raw, adjoint, top_factor, top_adjoint, inverse, input_sems, known_out, open_out, full, gathered, partial, pieces, moved, solved, slices, corner, tiles, columns, sums, terms, home,
    ring_send, ring_recv, twin_send, twin_recv, moved_send, moved_recv, sum_send, sum_recv,
    home_send, home_recv, slice_send, slice_recv, tile_send, tile_recv, term_send, term_recv, *spreads
):
    p, q = lax.axis_index("prow"), lax.axis_index("pcol")
    z, c = q // 2, lax.rem(q, 2)
    place = (p, z, c)
    known = Spread(known_out, NTOP, spreads[:7], place)
    opened = Spread(open_out, NBLK, spreads[7:], place)

    home_row, home_half = lax.rem(q, PROWS), q // PROWS

    loads = [
        pltpu.make_async_copy(src, dst, input_sems.at[i])
        for i, (src, dst) in enumerate([
            (factor_in, factor), (factor_top_in, top_factor), (inverse_in, inverse),
            (adjoint_in, adjoint_raw), (adjoint_top_in, top_adjoint),
        ])
    ]
    for load in loads:
        load.start()

    barrier = pltpu.get_barrier_semaphore()

    def greet(row, col):
        @pl.when((row != p) | (col != q))
        def _():
            pl.semaphore_signal(barrier, inc=1, device_id=(row, col), device_id_type=MESH)

    loop(1, PROWS, lambda step: greet(lax.rem(p + step, PROWS), q))
    loop(1, PCOLS, lambda step: greet(p, lax.rem(q + step, PCOLS)))
    for half in range(2):
        greet(z, half * PROWS + p)
        greet(home_row, 2 * p + half)
    loads[0].wait()
    for j in range(K):
        gathered[:, pl.ds(q, 1), :, j * NB : (j + 1) * NB] = factor[:, :, j][:, None]
    own = 1 // (1 + (z - p) * (z - p) + (home_row - p) * (home_row - p))
    pl.semaphore_wait(barrier, PROWS + PCOLS + 2 - 2 * own)

    steps = CHIPS // 2 - c

    def origin_of(step, core):
        return lax.rem(z + (CHIPS - step) * (1 - core) + step * core, CHIPS)

    def ring_copy(half, core, step, slot):
        part = gathered.at[half, origin_of(step, c) * 2 + core]
        peer = lax.rem(z + 1 + (CHIPS - 2) * c, CHIPS)
        return remote(
            part, part, ring_send.at[half, core, slot], ring_recv.at[half, core, slot], p, peer * 2 + c
        )

    def own_copy(core):
        part = gathered.at[:, z * 2 + core]
        return remote(part, part, twin_send.at[0], twin_recv.at[0], p, z * 2 + 1 - c)

    def twin_copy(step, core):
        part = gathered.at[:, pl.ds(origin_of(step, core) * 2, 2)]
        return remote(part, part, twin_send.at[step], twin_recv.at[step], p, z * 2 + 1 - c)

    for half in range(2):
        ring_copy(half, c, 0, 0).start()
    own_copy(c).start()
    loads[1].wait()
    loads[2].wait()

    @pl.when(p < NBLK)
    def _():
        known_out[pl.ds(p, 1), pl.ds(z, 1), pl.ds(c, 1)] = top_factor[pl.ds(lax.rem(p, NBLK), 1)][:, None, None]

    @pl.when((p >= NBLK) & (p < NTOP))
    def _():
        known_out[pl.ds(p, 1), pl.ds(z, 1), pl.ds(c, 1)] = inverse[pl.ds(lax.rem(p + 2, K), 1)][:, None, None]

    known.start_line()
    own_copy(1 - c).wait_recv()
    for half in range(2):
        ring_copy(half, 1 - c, 0, 0).start()
    loads[3].wait()
    for j in range(K):
        adjoint[:, :, j * NB : (j + 1) * NB] = adjoint_raw[:, :, j]

    def here_or_there(src, dst, send, recv, row, col, act):
        own = (row == p) & (col == q)

        @pl.when(own)
        def _():
            act(pltpu.make_async_copy(src, dst, recv), True)

        @pl.when(jnp.logical_not(own))
        def _():
            act(remote(src, dst, send, recv, row, col), False)

    def move_out(half, act):
        here_or_there(
            adjoint.at[half], moved.at[c], moved_send.at[half], moved_recv.at[c], z, half * PROWS + p, act
        )

    def start(copy, local):
        copy.start()

    def sent(copy, local):
        if not local:
            copy.wait_send()

    def arrived(copy, local):
        copy.wait() if local else copy.wait_recv()


    def ring_step(step):
        for core in (c, 1 - c):
            for half in range(2):
                ring_copy(half, core, step, step - 1).wait_recv()

                @pl.when(step < steps)
                def _():
                    ring_copy(half, core, step, step).start()

        twin_copy(step, c).start()

    loop(1, 4, ring_step)
    known.start_flat()
    loop(4, 7, ring_step)
    known.relay()
    loop(7, steps + 1, ring_step)
    loop(1, CHIPS // 2 + c, lambda step: twin_copy(step, 1 - c).wait_recv())

    for half in range(2):
        move_out(half, start)
    everything = gathered[...].reshape(2, NB, K * NB)
    image = inner_product(trail[0], everything[0]) + inner_product(trail[1], everything[1])
    partial[...] = image.reshape(PROWS, 16, K * NB)

    def sum_copy(step, source):
        target = lax.rem(p + step, PROWS)
        return remote(partial.at[target], pieces.at[source], sum_send.at[step], sum_recv.at[source], target, q)

    loop(1, PROWS, lambda index: sum_copy(far_first(index), p).start())
    pieces[pl.ds(p, 1)] = partial[pl.ds(p, 1)]

    loop(0, NTOP, known.share)
    loop(0, NTOP, known.finish)
    for half in range(2):
        here_or_there(
            adjoint.at[0], moved.at[half], moved_send.at[0], moved_recv.at[half], home_row, 2 * p + half, arrived
        )

    loop(1, PROWS, lambda step: sum_copy(step, lax.rem(p + step, PROWS)).wait_recv())
    total = pieces[0]
    for source in range(1, PROWS):
        total = total + pieces[source]
    residual = moved[...].reshape(16, K * NB) - 2.0 * total

    def block(slot):
        return known_out[slot].reshape(NB, NB)

    parts = [residual[:, j * NB : (j + 1) * NB] for j in range(K)]
    for j in reversed(range(K)):
        parts[j] = matmul(parts[j], block(NBLK + j))
        for earlier in range(j):
            parts[earlier] = parts[earlier] - matmul(parts[j], block(block_slot(j, earlier)))
        solved[:, :, j * NB : (j + 1) * NB] = parts[j].reshape(2, 8, NB)
        for side in range(2):
            slices[2 * j + side] = parts[j][:, side * 128 : (side + 1) * 128]

    base, spot = (p // 8) * 8, lax.rem(p, 8)

    def slice_copy(step, source):
        target = lax.rem(spot + step, 8)
        return remote(slices.at[target], corner.at[source], slice_send.at[step], slice_recv.at[source], base + target, q)

    loop(1, 8, lambda step: slice_copy(step, spot).start())
    corner[pl.ds(spot, 1)] = slices[pl.ds(spot, 1)]

    def home_out(half, act):
        here_or_there(
            solved.at[half], home.at[home_half], home_send.at[half], home_recv.at[home_half],
            home_row, 2 * p + half, act,
        )

    loop(1, 8, lambda step: slice_copy(step, lax.rem(spot + step, 8)).wait_recv())
    tiles[...] = corner[...].reshape(128, 128).T.reshape(16, 8, 128)

    panel, upper = spot // 2, lax.rem(spot, 2)
    quarter = home_half * 2 + p // 8

    def tile_out(k, act):
        here_or_there(
            tiles.at[k], columns.at[panel, quarter], tile_send.at[k], tile_recv.at[panel, quarter],
            home_row, upper * 16 + k, act,
        )

    loop(0, 16, lambda k: tile_out(lax.rem(k + p, 16), start))

    def tile_in(index):
        j, part = index // 4, lax.rem(index, 4)
        source_row = lax.rem(part, 2) * 8 + 2 * j + home_half
        source_col = (part // 2) * PROWS + p
        here_or_there(
            tiles.at[0], columns.at[j, part], tile_send.at[0], tile_recv.at[j, part], source_row, source_col, arrived
        )

    loop(0, 16, tile_in)
    wide = jnp.concatenate([columns[:, part].reshape(32, 128) for part in range(4)], axis=1)
    gram = matmul(wide, gathered[...].reshape(2 * NB, K * NB))
    for j in range(K):
        for i in range(j + 1):
            terms[block_slot(j, i)] = gram[j * 8 : (j + 1) * 8, i * NB : (i + 1) * NB]

    def term_copy(target, source):
        return remote(terms.at[target], sums.at[source], term_send.at[target], term_recv.at[source], target, q)

    def each_term(act):
        def body(step):
            target = lax.rem(p + step, PROWS)

            @pl.when(target < NBLK)
            def _():
                act(term_copy(target, p))

        loop(1, PROWS, body)

    each_term(lambda copy: copy.start())

    loads[4].wait()

    @pl.when(p < NBLK)
    def _():
        own = lax.rem(p, NBLK)
        sums[pl.ds(p, 1)] = terms[pl.ds(own, 1)]

        def body(step):
            source = lax.rem(p + step, PROWS)
            term_copy(own, source).wait_recv()

        loop(1, PROWS, body)
        whole = sums[0]
        for source in range(1, PROWS):
            whole = whole + sums[source]
        open_out[pl.ds(p, 1), pl.ds(z, 1), pl.ds(c, 1)] = (top_adjoint[own] - whole)[None, None, None]

    opened.start_line()
    opened.start_flat()
    opened.relay()

    def share_column(j):
        for r in range(j, K):
            opened.share(block_slot(r, j))

    share_column(K - 1)
    share_column(K - 2)
    for half in range(2):
        home_out(half, start)
    for j in reversed(range(K)):
        for r in range(j, K):
            opened.finish(block_slot(r, j))
        top_column(j, known_out, open_out, full)
        if j >= 2:
            share_column(j - 2)
    top_out[...] = full[:, pl.ds(pl.multiple_of(q * 8, 8), 8), :]
    for half in range(2):
        here_or_there(
            solved.at[0], home.at[half], home_send.at[0], home_recv.at[half], z, half * PROWS + p, arrived
        )
    low_out[...] = home[...]

    for half in range(2):
        for core in range(2):
            loop(0, steps, lambda step: ring_copy(half, core, step, step).wait_send())
    own_copy(c).wait_send()
    loop(1, steps + 1, lambda step: twin_copy(step, c).wait_send())
    for half in range(2):
        move_out(half, sent)
        home_out(half, sent)
    loop(1, PROWS, lambda step: sum_copy(step, p).wait_send())
    loop(1, 8, lambda step: slice_copy(step, spot).wait_send())
    loop(0, 16, lambda k: tile_out(k, sent))
    each_term(lambda copy: copy.wait_send())
    known.drain()
    opened.drain()


def half_lower(square):
    row_ids = lax.broadcasted_iota(jnp.int32, (NB, NB), 0)
    col_ids = lax.broadcasted_iota(jnp.int32, (NB, NB), 1)
    return jnp.where(row_ids > col_ids, square, jnp.where(row_ids == col_ids, 0.5 * square, 0.0))


def lower(square):
    row_ids = lax.broadcasted_iota(jnp.int32, (NB, NB), 0)
    col_ids = lax.broadcasted_iota(jnp.int32, (NB, NB), 1)
    return jnp.where(row_ids >= col_ids, square, 0.0)


def top_column(j, known, opened, full):
    def factor(r, j):
        return known[block_slot(r, j)].reshape(NB, NB)

    def grad(r, j):
        return full[block_slot(r, j)]

    inverse = known[NBLK + j].reshape(NB, NB)
    for r in range(j + 1, K):
        rest = opened[block_slot(r, j)].reshape(NB, NB) - 2.0 * matmul(grad(r, r), factor(r, j))
        for middle in range(j + 1, r):
            rest = rest - matmul(grad(r, middle), factor(middle, j))
        for beyond in range(r + 1, K):
            rest = rest - inner_product(grad(beyond, r), factor(beyond, j))
        full[block_slot(r, j)] = matmul(rest, inverse)
    adj = opened[block_slot(j, j)].reshape(NB, NB)
    for r in range(j + 1, K):
        adj = adj - inner_product(grad(r, j), factor(r, j))
    inner = half_lower(inner_product(lower(factor(j, j)), lower(adj)))
    spread = inner_product(inverse, matmul(inner, inverse))
    full[block_slot(j, j)] = 0.5 * (spread + spread.T)


def per_device(adjoint_trail, factor_low, adjoint_low, factor_top, adjoint_top, diag_inverse):
    dma = pltpu.SemaphoreType.DMA
    vmem = pl.BlockSpec(memory_space=pltpu.VMEM)
    wide = K * NB
    low_grad, grad_top = pl.pallas_call(
        exchange_kernel,
        out_shape=[
            jax.ShapeDtypeStruct((2, 8, wide), F32),
            jax.ShapeDtypeStruct((NBLK, 8, NB), F32),
        ],
        in_specs=[vmem] + [pl.BlockSpec(memory_space=pltpu.MemorySpace.HBM)] * 5,
        out_specs=[vmem] * 2,
        scratch_shapes=[
            pltpu.VMEM((2, 8, K, NB), F32),
            pltpu.VMEM((2, 8, K, NB), F32),
            pltpu.VMEM((2, 8, wide), F32),
            pltpu.VMEM((NBLK, 8, NB), F32),
            pltpu.VMEM((NBLK, 8, NB), F32),
            pltpu.VMEM((K, 8, NB), F32),
            dma((5,)),
            pltpu.VMEM((NTOP, CHIPS, 2, 8, NB), F32),
            pltpu.VMEM((NBLK, CHIPS, 2, 8, NB), F32),
            pltpu.VMEM((NBLK, NB, NB), F32),
            pltpu.VMEM((2, PCOLS, 8, wide), F32),
            pltpu.VMEM((PROWS, 16, wide), F32),
            pltpu.VMEM((PROWS, 16, wide), F32),
            pltpu.VMEM((2, 8, wide), F32),
            pltpu.VMEM((2, 8, wide), F32),
            pltpu.VMEM((8, 16, 128), F32),
            pltpu.VMEM((8, 16, 128), F32),
            pltpu.VMEM((16, 8, 128), F32),
            pltpu.VMEM((4, 4, 8, 128), F32),
            pltpu.VMEM((PROWS, 8, NB), F32),
            pltpu.VMEM((NBLK, 8, NB), F32),
            pltpu.VMEM((2, 8, wide), F32),
            dma((2, 2, 8)), dma((2, 2, 8)), dma((9,)), dma((9,)), dma((2,)), dma((2,)),
            dma((PROWS,)), dma((PROWS,)), dma((2,)), dma((2,)), dma((8,)), dma((8,)),
            dma((16,)), dma((4, 4)), dma((NBLK,)), dma((PROWS,)),
            *spread_sems(NTOP),
            *spread_sems(NBLK),
        ],
        compiler_params=pltpu.CompilerParams(collective_id=0, has_side_effects=True, vmem_limit_bytes=40 * 1024 * 1024),
        name="exchange",
    )(
        adjoint_trail.reshape(2, NB, NB),
        factor_low.reshape(2, 8, K, NB),
        adjoint_low.reshape(2, 8, K, NB),
        factor_top,
        adjoint_top,
        diag_inverse,
    )
    return low_grad.reshape(factor_low.shape), grad_top


def solution(mesh):
    in_specs = (
        P(None, "prow", None, None, "pcol", None),
        P(None, "prow", "pcol", None, None, None),
        P(None, "prow", "pcol", None, None, None),
        P(None, "pcol", None),
        P(None, "pcol", None),
        P(None, "pcol", None),
    )
    out_specs = (P(None, "prow", "pcol", None, None, None), P(None, "pcol", None))
    return jax.shard_map(
        per_device, mesh=mesh, in_specs=in_specs, out_specs=out_specs, check_vma=False
    )
```

```python
import jax
import jax.numpy as jnp
from jax import lax
from jax.experimental import pallas as pl
from jax.experimental.pallas import tpu as pltpu
from jax.sharding import PartitionSpec as P

NB = 256
K = 4
NBLK = 10
NTOP = NBLK + K
PROWS = 16
PCOLS = 32
CHIPS = 16
SIDE = 4

MESH = pl.DeviceIdType.MESH
F32 = jnp.float32
BF16 = jnp.bfloat16


def split(array):
    high = array.astype(BF16)
    return high, (array - high.astype(F32)).astype(BF16)


def product(left, right, dims):
    (a, a_rest), (b, b_rest) = split(left), split(right)

    def dot(x, y):
        return lax.dot_general(x, y, (dims, ((), ())), preferred_element_type=F32)

    return dot(a, b) + (dot(a, b_rest) + dot(a_rest, b))


def matmul(left, right):
    return product(left, right, ((1,), (0,)))


def inner_product(left, right):
    return product(left, right, ((0,), (0,)))


def block_slot(row_block, col_block):
    return row_block * (row_block + 1) // 2 + col_block


def loop(low, high, body):
    lax.fori_loop(low, high, lambda i, carry: (body(i), carry)[1], 0)


def remote(src, dst, send, recv, row, col):
    return pltpu.make_async_remote_copy(
        src_ref=src, dst_ref=dst, send_sem=send, recv_sem=recv, device_id=(row, col), device_id_type=MESH
    )


def far_first(index):
    rest = CHIPS - index
    odd = lax.rem(rest, 2)
    return (rest // 2 + 1) * odd + (CHIPS - rest // 2) * (1 - odd)


class Spread:
    def __init__(self, buf, count, sems, place):
        self.buf, self.count, self.place = buf, count, place
        self.line_send, self.line_recv, self.near_send, self.far_send, self.flat_recv, self.twin_send, self.twin_recv = sems

    def line_copy(self, step, origin):
        p, z, c = self.place
        tile = self.buf.at[p, origin, c]
        peer = lax.rem(z + step, CHIPS) * 2 + c
        return remote(tile, tile, self.line_send.at[step], self.line_recv.at[origin], p, peer)

    def peers(self, step):
        p, z, c = self.place
        x, y = p // SIDE, lax.rem(p, SIDE)
        along_x = lax.rem(x + step, SIDE) * SIDE + y
        along_y = x * SIDE + lax.rem(y + step, SIDE)
        return along_x * (1 - c) + along_y * c, along_y * (1 - c) + along_x * c

    def near_copy(self, step):
        p, z, c = self.place
        half = self.buf.at[p, :, c]
        return remote(half, half, self.near_send.at[step], self.flat_recv.at[p], self.peers(step)[0], z * 2 + c)

    def far_copy(self, block, origin, step):
        p, z, c = self.place
        half = self.buf.at[block, :, c]
        return remote(
            half, half, self.far_send.at[origin, step], self.flat_recv.at[block], self.peers(step)[1], z * 2 + c
        )

    def twin_copy(self, block, core):
        p, z, c = self.place
        half = self.buf.at[block, :, core]
        return remote(half, half, self.twin_send.at[block], self.twin_recv.at[block], p, z * 2 + 1 - c)

    def start_line(self):
        p, z, c = self.place

        @pl.when(p < self.count)
        def _():
            loop(1, CHIPS, lambda index: self.line_copy(far_first(index), z).start())

    def start_flat(self):
        p, z, c = self.place

        @pl.when(p < self.count)
        def _():
            loop(1, CHIPS, lambda step: self.line_copy(step, lax.rem(z + step, CHIPS)).wait_recv())

            def body(step):
                self.near_copy(step).start()
                self.far_copy(p, 0, step).start()

            loop(1, SIDE, body)
            self.twin_copy(p, c).start()

    def relay(self):
        def body(origin):
            block = self.peers(origin)[0]

            @pl.when(block < self.count)
            def _():
                self.far_copy(block, origin, 1).wait_recv()
                loop(1, SIDE, lambda step: self.far_copy(block, origin, step).start())

        loop(1, SIDE, body)

    def share(self, block):
        p, z, c = self.place
        x, y = p // SIDE, lax.rem(p, SIDE)
        straight = (block // SIDE) * (1 - c) + lax.rem(block, SIDE) * c
        mine = x * (1 - c) + y * c
        cross = lax.rem(block, SIDE) * (1 - c) + (block // SIDE) * c
        level = y * (1 - c) + x * c

        @pl.when(block != p)
        def _():
            @pl.when((straight == mine) | (cross != level))
            def _():
                self.far_copy(block, 0, 1).wait_recv()

            self.twin_copy(block, c).start()

    def finish(self, block):
        p, z, c = self.place
        self.twin_copy(block, 1 - c).wait_recv()

    def drain(self):
        p, z, c = self.place

        @pl.when(p < self.count)
        def _():
            loop(1, CHIPS, lambda step: self.line_copy(step, z).wait_send())

            def body(step):
                self.near_copy(step).wait_send()
                self.far_copy(p, 0, step).wait_send()

            loop(1, SIDE, body)

        def relayed(origin):
            block = self.peers(origin)[0]

            @pl.when(block < self.count)
            def _():
                loop(1, SIDE, lambda step: self.far_copy(block, origin, step).wait_send())

        loop(1, SIDE, relayed)
        loop(0, self.count, lambda block: self.twin_copy(block, c).wait_send())


def spread_sems(count):
    dma = pltpu.SemaphoreType.DMA
    return [
        dma((CHIPS,)), dma((CHIPS,)), dma((SIDE,)), dma((SIDE, SIDE)), dma((PROWS,)), dma((count,)), dma((count,))
    ]


def exchange_kernel(
    trail, factor_in, adjoint_in, factor_top_in, adjoint_top_in, inverse_in, low_out, top_out,
    factor, adjoint_raw, adjoint, top_factor, top_adjoint, inverse, input_sems, known_out, open_out, full, gathered, partial, pieces, moved, solved, slices, corner, tiles, columns, sums, terms, home,
    ring_send, ring_recv, twin_send, twin_recv, moved_send, moved_recv, sum_send, sum_recv,
    home_send, home_recv, slice_send, slice_recv, tile_send, tile_recv, term_send, term_recv, *spreads
):
    p, q = lax.axis_index("prow"), lax.axis_index("pcol")
    z, c = q // 2, lax.rem(q, 2)
    place = (p, z, c)
    known = Spread(known_out, NTOP, spreads[:7], place)
    opened = Spread(open_out, NBLK, spreads[7:], place)

    home_row, home_half = lax.rem(q, PROWS), q // PROWS

    loads = [
        pltpu.make_async_copy(src, dst, input_sems.at[i])
        for i, (src, dst) in enumerate([
            (factor_in, factor), (factor_top_in, top_factor), (inverse_in, inverse),
            (adjoint_in, adjoint_raw), (adjoint_top_in, top_adjoint),
        ])
    ]
    for load in loads:
        load.start()

    barrier = pltpu.get_barrier_semaphore()

    def greet(row, col):
        @pl.when((row != p) | (col != q))
        def _():
            pl.semaphore_signal(barrier, inc=1, device_id=(row, col), device_id_type=MESH)

    loop(1, PROWS, lambda step: greet(lax.rem(p + step, PROWS), q))
    loop(1, PCOLS, lambda step: greet(p, lax.rem(q + step, PCOLS)))
    for half in range(2):
        greet(z, half * PROWS + p)
        greet(home_row, 2 * p + half)
    loads[0].wait()
    for j in range(K):
        gathered[:, pl.ds(q, 1), :, j * NB : (j + 1) * NB] = factor[:, :, j][:, None]
    own = 1 // (1 + (z - p) * (z - p) + (home_row - p) * (home_row - p))
    pl.semaphore_wait(barrier, PROWS + PCOLS + 2 - 2 * own)

    steps = CHIPS // 2 - c

    def origin_of(step, core):
        return lax.rem(z + (CHIPS - step) * (1 - core) + step * core, CHIPS)

    def ring_copy(half, core, step, slot):
        part = gathered.at[half, origin_of(step, c) * 2 + core]
        peer = lax.rem(z + 1 + (CHIPS - 2) * c, CHIPS)
        return remote(
            part, part, ring_send.at[half, core, slot], ring_recv.at[half, core, slot], p, peer * 2 + c
        )

    def own_copy(core):
        part = gathered.at[:, z * 2 + core]
        return remote(part, part, twin_send.at[0], twin_recv.at[0], p, z * 2 + 1 - c)

    def twin_copy(step, core):
        part = gathered.at[:, pl.ds(origin_of(step, core) * 2, 2)]
        return remote(part, part, twin_send.at[step], twin_recv.at[step], p, z * 2 + 1 - c)

    for half in range(2):
        ring_copy(half, c, 0, 0).start()
    own_copy(c).start()
    loads[1].wait()
    loads[2].wait()

    @pl.when(p < NBLK)
    def _():
        known_out[pl.ds(p, 1), pl.ds(z, 1), pl.ds(c, 1)] = top_factor[pl.ds(lax.rem(p, NBLK), 1)][:, None, None]

    @pl.when((p >= NBLK) & (p < NTOP))
    def _():
        known_out[pl.ds(p, 1), pl.ds(z, 1), pl.ds(c, 1)] = inverse[pl.ds(lax.rem(p + 2, K), 1)][:, None, None]

    known.start_line()
    own_copy(1 - c).wait_recv()
    for half in range(2):
        ring_copy(half, 1 - c, 0, 0).start()
    loads[3].wait()
    for j in range(K):
        adjoint[:, :, j * NB : (j + 1) * NB] = adjoint_raw[:, :, j]

    def here_or_there(src, dst, send, recv, row, col, act):
        own = (row == p) & (col == q)

        @pl.when(own)
        def _():
            act(pltpu.make_async_copy(src, dst, recv), True)

        @pl.when(jnp.logical_not(own))
        def _():
            act(remote(src, dst, send, recv, row, col), False)

    def move_out(half, act):
        here_or_there(
            adjoint.at[half], moved.at[c], moved_send.at[half], moved_recv.at[c], z, half * PROWS + p, act
        )

    def start(copy, local):
        copy.start()

    def sent(copy, local):
        if not local:
            copy.wait_send()

    def arrived(copy, local):
        copy.wait() if local else copy.wait_recv()


    def ring_step(step):
        for core in (c, 1 - c):
            for half in range(2):
                ring_copy(half, core, step, step - 1).wait_recv()

                @pl.when(step < steps)
                def _():
                    ring_copy(half, core, step, step).start()

        twin_copy(step, c).start()

    loop(1, 4, ring_step)
    known.start_flat()
    loop(4, 7, ring_step)
    known.relay()
    loop(7, steps + 1, ring_step)
    loop(1, CHIPS // 2 + c, lambda step: twin_copy(step, 1 - c).wait_recv())

    for half in range(2):
        move_out(half, start)
    everything = gathered[...].reshape(2, NB, K * NB)
    image = inner_product(trail[0], everything[0]) + inner_product(trail[1], everything[1])
    partial[...] = image.reshape(PROWS, 16, K * NB)

    def sum_copy(step, source):
        target = lax.rem(p + step, PROWS)
        return remote(partial.at[target], pieces.at[source], sum_send.at[step], sum_recv.at[source], target, q)

    loop(1, PROWS, lambda index: sum_copy(far_first(index), p).start())
    pieces[pl.ds(p, 1)] = partial[pl.ds(p, 1)]

    loop(0, NTOP, known.share)
    loop(0, NTOP, known.finish)
    for half in range(2):
        here_or_there(
            adjoint.at[0], moved.at[half], moved_send.at[0], moved_recv.at[half], home_row, 2 * p + half, arrived
        )

    loop(1, PROWS, lambda step: sum_copy(step, lax.rem(p + step, PROWS)).wait_recv())
    total = pieces[0]
    for source in range(1, PROWS):
        total = total + pieces[source]
    residual = moved[...].reshape(16, K * NB) - 2.0 * total

    def block(slot):
        return known_out[slot].reshape(NB, NB)

    parts = [residual[:, j * NB : (j + 1) * NB] for j in range(K)]
    for j in reversed(range(K)):
        parts[j] = matmul(parts[j], block(NBLK + j))
        for earlier in range(j):
            parts[earlier] = parts[earlier] - matmul(parts[j], block(block_slot(j, earlier)))
        solved[:, :, j * NB : (j + 1) * NB] = parts[j].reshape(2, 8, NB)
        for side in range(2):
            slices[2 * j + side] = parts[j][:, side * 128 : (side + 1) * 128]

    base, spot = (p // 8) * 8, lax.rem(p, 8)

    def slice_copy(step, source):
        target = lax.rem(spot + step, 8)
        return remote(slices.at[target], corner.at[source], slice_send.at[step], slice_recv.at[source], base + target, q)

    loop(1, 8, lambda step: slice_copy(step, spot).start())
    corner[pl.ds(spot, 1)] = slices[pl.ds(spot, 1)]

    def home_out(half, act):
        here_or_there(
            solved.at[half], home.at[home_half], home_send.at[half], home_recv.at[home_half],
            home_row, 2 * p + half, act,
        )

    loop(1, 8, lambda step: slice_copy(step, lax.rem(spot + step, 8)).wait_recv())
    tiles[...] = corner[...].reshape(128, 128).T.reshape(16, 8, 128)

    panel, upper = spot // 2, lax.rem(spot, 2)
    quarter = home_half * 2 + p // 8

    def tile_out(k, act):
        here_or_there(
            tiles.at[k], columns.at[panel, quarter], tile_send.at[k], tile_recv.at[panel, quarter],
            home_row, upper * 16 + k, act,
        )

    loop(0, 16, lambda k: tile_out(lax.rem(k + p, 16), start))

    def tile_in(index):
        j, part = index // 4, lax.rem(index, 4)
        source_row = lax.rem(part, 2) * 8 + 2 * j + home_half
        source_col = (part // 2) * PROWS + p
        here_or_there(
            tiles.at[0], columns.at[j, part], tile_send.at[0], tile_recv.at[j, part], source_row, source_col, arrived
        )

    loop(0, 16, tile_in)
    wide = jnp.concatenate([columns[:, part].reshape(32, 128) for part in range(4)], axis=1)
    gram = matmul(wide, gathered[...].reshape(2 * NB, K * NB))
    for j in range(K):
        for i in range(j + 1):
            terms[block_slot(j, i)] = gram[j * 8 : (j + 1) * 8, i * NB : (i + 1) * NB]

    def term_copy(target, source):
        return remote(terms.at[target], sums.at[source], term_send.at[target], term_recv.at[source], target, q)

    def each_term(act):
        def body(step):
            target = lax.rem(p + step, PROWS)

            @pl.when(target < NBLK)
            def _():
                act(term_copy(target, p))

        loop(1, PROWS, body)

    each_term(lambda copy: copy.start())

    loads[4].wait()

    @pl.when(p < NBLK)
    def _():
        own = lax.rem(p, NBLK)
        sums[pl.ds(p, 1)] = terms[pl.ds(own, 1)]

        def body(step):
            source = lax.rem(p + step, PROWS)
            term_copy(own, source).wait_recv()

        loop(1, PROWS, body)
        whole = sums[0]
        for source in range(1, PROWS):
            whole = whole + sums[source]
        open_out[pl.ds(p, 1), pl.ds(z, 1), pl.ds(c, 1)] = (top_adjoint[own] - whole)[None, None, None]

    opened.start_line()
    opened.start_flat()
    opened.relay()

    def share_column(j):
        for r in range(j, K):
            opened.share(block_slot(r, j))

    share_column(K - 1)
    share_column(K - 2)
    for half in range(2):
        home_out(half, start)
    for j in reversed(range(K)):
        for r in range(j, K):
            opened.finish(block_slot(r, j))
        top_column(j, known_out, open_out, full)
        if j >= 2:
            share_column(j - 2)
    top_out[...] = full[:, pl.ds(pl.multiple_of(q * 8, 8), 8), :]
    for half in range(2):
        here_or_there(
            solved.at[0], home.at[half], home_send.at[0], home_recv.at[half], z, half * PROWS + p, arrived
        )
    low_out[...] = home[...]

    for half in range(2):
        for core in range(2):
            loop(0, steps, lambda step: ring_copy(half, core, step, step).wait_send())
    own_copy(c).wait_send()
    loop(1, steps + 1, lambda step: twin_copy(step, c).wait_send())
    for half in range(2):
        move_out(half, sent)
        home_out(half, sent)
    loop(1, PROWS, lambda step: sum_copy(step, p).wait_send())
    loop(1, 8, lambda step: slice_copy(step, spot).wait_send())
    loop(0, 16, lambda k: tile_out(k, sent))
    each_term(lambda copy: copy.wait_send())
    known.drain()
    opened.drain()


def half_lower(square):
    row_ids = lax.broadcasted_iota(jnp.int32, (NB, NB), 0)
    col_ids = lax.broadcasted_iota(jnp.int32, (NB, NB), 1)
    return jnp.where(row_ids > col_ids, square, jnp.where(row_ids == col_ids, 0.5 * square, 0.0))


def lower(square):
    row_ids = lax.broadcasted_iota(jnp.int32, (NB, NB), 0)
    col_ids = lax.broadcasted_iota(jnp.int32, (NB, NB), 1)
    return jnp.where(row_ids >= col_ids, square, 0.0)


def top_column(j, known, opened, full):
    def factor(r, j):
        return known[block_slot(r, j)].reshape(NB, NB)

    def grad(r, j):
        return full[block_slot(r, j)]

    inverse = known[NBLK + j].reshape(NB, NB)
    for r in range(j + 1, K):
        rest = opened[block_slot(r, j)].reshape(NB, NB) - 2.0 * matmul(grad(r, r), factor(r, j))
        for middle in range(j + 1, r):
            rest = rest - matmul(grad(r, middle), factor(middle, j))
        for beyond in range(r + 1, K):
            rest = rest - inner_product(grad(beyond, r), factor(beyond, j))
        full[block_slot(r, j)] = matmul(rest, inverse)
    adj = opened[block_slot(j, j)].reshape(NB, NB)
    for r in range(j + 1, K):
        adj = adj - inner_product(grad(r, j), factor(r, j))
    inner = half_lower(inner_product(lower(factor(j, j)), lower(adj)))
    spread = inner_product(inverse, matmul(inner, inverse))
    full[block_slot(j, j)] = 0.5 * (spread + spread.T)


def per_device(adjoint_trail, factor_low, adjoint_low, factor_top, adjoint_top, diag_inverse):
    dma = pltpu.SemaphoreType.DMA
    vmem = pl.BlockSpec(memory_space=pltpu.VMEM)
    wide = K * NB
    low_grad, grad_top = pl.pallas_call(
        exchange_kernel,
        out_shape=[
            jax.ShapeDtypeStruct((2, 8, wide), F32),
            jax.ShapeDtypeStruct((NBLK, 8, NB), F32),
        ],
        in_specs=[vmem] + [pl.BlockSpec(memory_space=pltpu.MemorySpace.HBM)] * 5,
        out_specs=[vmem] * 2,
        scratch_shapes=[
            pltpu.VMEM((2, 8, K, NB), F32),
            pltpu.VMEM((2, 8, K, NB), F32),
            pltpu.VMEM((2, 8, wide), F32),
            pltpu.VMEM((NBLK, 8, NB), F32),
            pltpu.VMEM((NBLK, 8, NB), F32),
            pltpu.VMEM((K, 8, NB), F32),
            dma((5,)),
            pltpu.VMEM((NTOP, CHIPS, 2, 8, NB), F32),
            pltpu.VMEM((NBLK, CHIPS, 2, 8, NB), F32),
            pltpu.VMEM((NBLK, NB, NB), F32),
            pltpu.VMEM((2, PCOLS, 8, wide), F32),
            pltpu.VMEM((PROWS, 16, wide), F32),
            pltpu.VMEM((PROWS, 16, wide), F32),
            pltpu.VMEM((2, 8, wide), F32),
            pltpu.VMEM((2, 8, wide), F32),
            pltpu.VMEM((8, 16, 128), F32),
            pltpu.VMEM((8, 16, 128), F32),
            pltpu.VMEM((16, 8, 128), F32),
            pltpu.VMEM((4, 4, 8, 128), F32),
            pltpu.VMEM((PROWS, 8, NB), F32),
            pltpu.VMEM((NBLK, 8, NB), F32),
            pltpu.VMEM((2, 8, wide), F32),
            dma((2, 2, 8)), dma((2, 2, 8)), dma((9,)), dma((9,)), dma((2,)), dma((2,)),
            dma((PROWS,)), dma((PROWS,)), dma((2,)), dma((2,)), dma((8,)), dma((8,)),
            dma((16,)), dma((4, 4)), dma((NBLK,)), dma((PROWS,)),
            *spread_sems(NTOP),
            *spread_sems(NBLK),
        ],
        compiler_params=pltpu.CompilerParams(collective_id=0, has_side_effects=True, vmem_limit_bytes=40 * 1024 * 1024),
        name="exchange",
    )(
        adjoint_trail.reshape(2, NB, NB),
        factor_low.reshape(2, 8, K, NB),
        adjoint_low.reshape(2, 8, K, NB),
        factor_top,
        adjoint_top,
        diag_inverse,
    )
    return low_grad.reshape(factor_low.shape), grad_top


def solution(mesh):
    in_specs = (
        P(None, "prow", None, None, "pcol", None),
        P(None, "prow", "pcol", None, None, None),
        P(None, "prow", "pcol", None, None, None),
        P(None, "pcol", None),
        P(None, "pcol", None),
        P(None, "pcol", None),
    )
    out_specs = (P(None, "prow", "pcol", None, None, None), P(None, "pcol", None))
    return jax.shard_map(
        per_device, mesh=mesh, in_specs=in_specs, out_specs=out_specs, check_vma=False
    )
```

```python
import jax
import jax.numpy as jnp
from jax import lax
from jax.experimental import pallas as pl
from jax.experimental.pallas import tpu as pltpu
from jax.sharding import PartitionSpec as P

NB = 256
K = 4
NBLK = 10
NTOP = NBLK + K
PROWS = 16
PCOLS = 32
CHIPS = 16
SIDE = 4

MESH = pl.DeviceIdType.MESH
F32 = jnp.float32
BF16 = jnp.bfloat16


def split(array):
    high = array.astype(BF16)
    return high, (array - high.astype(F32)).astype(BF16)


def product(left, right, dims):
    (a, a_rest), (b, b_rest) = split(left), split(right)

    def dot(x, y):
        return lax.dot_general(x, y, (dims, ((), ())), preferred_element_type=F32)

    return dot(a, b) + (dot(a, b_rest) + dot(a_rest, b))


def matmul(left, right):
    return product(left, right, ((1,), (0,)))


def inner_product(left, right):
    return product(left, right, ((0,), (0,)))


def block_slot(row_block, col_block):
    return row_block * (row_block + 1) // 2 + col_block


def loop(low, high, body):
    lax.fori_loop(low, high, lambda i, carry: (body(i), carry)[1], 0)


def remote(src, dst, send, recv, row, col):
    return pltpu.make_async_remote_copy(
        src_ref=src, dst_ref=dst, send_sem=send, recv_sem=recv, device_id=(row, col), device_id_type=MESH
    )


def far_first(index):
    rest = CHIPS - index
    odd = lax.rem(rest, 2)
    return (rest // 2 + 1) * odd + (CHIPS - rest // 2) * (1 - odd)


class Spread:
    def __init__(self, buf, count, sems, place):
        self.buf, self.count, self.place = buf, count, place
        self.line_send, self.line_recv, self.near_send, self.far_send, self.flat_recv, self.twin_send, self.twin_recv = sems

    def line_copy(self, step, origin):
        p, z, c = self.place
        tile = self.buf.at[p, origin, c]
        peer = lax.rem(z + step, CHIPS) * 2 + c
        return remote(tile, tile, self.line_send.at[step], self.line_recv.at[origin], p, peer)

    def peers(self, step):
        p, z, c = self.place
        x, y = p // SIDE, lax.rem(p, SIDE)
        along_x = lax.rem(x + step, SIDE) * SIDE + y
        along_y = x * SIDE + lax.rem(y + step, SIDE)
        return along_x * (1 - c) + along_y * c, along_y * (1 - c) + along_x * c

    def near_copy(self, step):
        p, z, c = self.place
        half = self.buf.at[p, :, c]
        return remote(half, half, self.near_send.at[step], self.flat_recv.at[p], self.peers(step)[0], z * 2 + c)

    def far_copy(self, block, origin, step):
        p, z, c = self.place
        half = self.buf.at[block, :, c]
        return remote(
            half, half, self.far_send.at[origin, step], self.flat_recv.at[block], self.peers(step)[1], z * 2 + c
        )

    def twin_copy(self, block, core):
        p, z, c = self.place
        half = self.buf.at[block, :, core]
        return remote(half, half, self.twin_send.at[block], self.twin_recv.at[block], p, z * 2 + 1 - c)

    def start_line(self):
        p, z, c = self.place

        @pl.when(p < self.count)
        def _():
            loop(1, CHIPS, lambda index: self.line_copy(far_first(index), z).start())

    def start_flat(self):
        p, z, c = self.place

        @pl.when(p < self.count)
        def _():
            loop(1, CHIPS, lambda step: self.line_copy(step, lax.rem(z + step, CHIPS)).wait_recv())

            for step in (1, 3, 2):
                self.near_copy(step).start()
            for step in (1, 3, 2):
                self.far_copy(p, 0, step).start()
            self.twin_copy(p, c).start()

    def relay(self):
        def body(origin):
            block = self.peers(origin)[0]

            @pl.when(block < self.count)
            def _():
                self.far_copy(block, origin, 1).wait_recv()
                for step in (1, 3, 2):
                    self.far_copy(block, origin, step).start()

        for origin in (1, 3, 2):
            body(origin)

    def share(self, block):
        p, z, c = self.place
        x, y = p // SIDE, lax.rem(p, SIDE)
        straight = (block // SIDE) * (1 - c) + lax.rem(block, SIDE) * c
        mine = x * (1 - c) + y * c
        cross = lax.rem(block, SIDE) * (1 - c) + (block // SIDE) * c
        level = y * (1 - c) + x * c

        @pl.when(block != p)
        def _():
            @pl.when((straight == mine) | (cross != level))
            def _():
                self.far_copy(block, 0, 1).wait_recv()

            self.twin_copy(block, c).start()

    def finish(self, block):
        p, z, c = self.place
        self.twin_copy(block, 1 - c).wait_recv()

    def drain(self):
        p, z, c = self.place

        @pl.when(p < self.count)
        def _():
            loop(1, CHIPS, lambda step: self.line_copy(step, z).wait_send())

            def body(step):
                self.near_copy(step).wait_send()
                self.far_copy(p, 0, step).wait_send()

            loop(1, SIDE, body)

        def relayed(origin):
            block = self.peers(origin)[0]

            @pl.when(block < self.count)
            def _():
                loop(1, SIDE, lambda step: self.far_copy(block, origin, step).wait_send())

        loop(1, SIDE, relayed)
        loop(0, self.count, lambda block: self.twin_copy(block, c).wait_send())


def spread_sems(count):
    dma = pltpu.SemaphoreType.DMA
    return [
        dma((CHIPS,)), dma((CHIPS,)), dma((SIDE,)), dma((SIDE, SIDE)), dma((PROWS,)), dma((count,)), dma((count,))
    ]


def exchange_kernel(
    trail, factor_in, adjoint_in, factor_top_in, adjoint_top_in, inverse_in, low_out, top_out,
    factor, adjoint_raw, adjoint, top_factor, top_adjoint, inverse, input_sems, known_out, open_out, full, gathered, partial, pieces, moved, solved, slices, corner, tiles, columns, sums, terms, home,
    ring_send, ring_recv, twin_send, twin_recv, moved_send, moved_recv, sum_send, sum_recv,
    home_send, home_recv, slice_send, slice_recv, tile_send, tile_recv, term_send, term_recv, *spreads
):
    p, q = lax.axis_index("prow"), lax.axis_index("pcol")
    z, c = q // 2, lax.rem(q, 2)
    place = (p, z, c)
    known = Spread(known_out, NTOP, spreads[:7], place)
    opened = Spread(open_out, NBLK, spreads[7:], place)

    home_row, home_half = lax.rem(q, PROWS), q // PROWS

    loads = [
        pltpu.make_async_copy(src, dst, input_sems.at[i])
        for i, (src, dst) in enumerate([
            (factor_in, factor), (factor_top_in, top_factor), (inverse_in, inverse),
            (adjoint_in, adjoint_raw), (adjoint_top_in, top_adjoint),
        ])
    ]
    for load in loads:
        load.start()

    barrier = pltpu.get_barrier_semaphore()

    def greet(row, col):
        @pl.when((row != p) | (col != q))
        def _():
            pl.semaphore_signal(barrier, inc=1, device_id=(row, col), device_id_type=MESH)

    loop(1, PROWS, lambda step: greet(lax.rem(p + step, PROWS), q))
    loop(1, PCOLS, lambda step: greet(p, lax.rem(q + step, PCOLS)))
    for half in range(2):
        greet(z, half * PROWS + p)
        greet(home_row, 2 * p + half)
    loads[0].wait()
    for j in range(K):
        gathered[:, pl.ds(q, 1), :, j * NB : (j + 1) * NB] = factor[:, :, j][:, None]
    own = 1 // (1 + (z - p) * (z - p) + (home_row - p) * (home_row - p))
    pl.semaphore_wait(barrier, PROWS + PCOLS + 2 - 2 * own)

    steps = CHIPS // 2 - c

    def origin_of(step, core):
        return lax.rem(z + (CHIPS - step) * (1 - core) + step * core, CHIPS)

    def ring_copy(half, core, step, slot):
        part = gathered.at[half, origin_of(step, c) * 2 + core]
        peer = lax.rem(z + 1 + (CHIPS - 2) * c, CHIPS)
        return remote(
            part, part, ring_send.at[half, core, slot], ring_recv.at[half, core, slot], p, peer * 2 + c
        )

    def own_copy(core):
        part = gathered.at[:, z * 2 + core]
        return remote(part, part, twin_send.at[0], twin_recv.at[0], p, z * 2 + 1 - c)

    def twin_copy(step, core):
        part = gathered.at[:, pl.ds(origin_of(step, core) * 2, 2)]
        return remote(part, part, twin_send.at[step], twin_recv.at[step], p, z * 2 + 1 - c)

    for half in range(2):
        ring_copy(half, c, 0, 0).start()
    own_copy(c).start()
    loads[1].wait()
    loads[2].wait()

    @pl.when(p < NBLK)
    def _():
        known_out[pl.ds(p, 1), pl.ds(z, 1), pl.ds(c, 1)] = top_factor[pl.ds(lax.rem(p, NBLK), 1)][:, None, None]

    @pl.when((p >= NBLK) & (p < NTOP))
    def _():
        known_out[pl.ds(p, 1), pl.ds(z, 1), pl.ds(c, 1)] = inverse[pl.ds(lax.rem(p + 2, K), 1)][:, None, None]

    known.start_line()
    own_copy(1 - c).wait_recv()
    for half in range(2):
        ring_copy(half, 1 - c, 0, 0).start()
    loads[3].wait()
    for j in range(K):
        adjoint[:, :, j * NB : (j + 1) * NB] = adjoint_raw[:, :, j]

    def here_or_there(src, dst, send, recv, row, col, act):
        own = (row == p) & (col == q)

        @pl.when(own)
        def _():
            act(pltpu.make_async_copy(src, dst, recv), True)

        @pl.when(jnp.logical_not(own))
        def _():
            act(remote(src, dst, send, recv, row, col), False)

    def move_out(half, act):
        here_or_there(
            adjoint.at[half], moved.at[c], moved_send.at[half], moved_recv.at[c], z, half * PROWS + p, act
        )

    def start(copy, local):
        copy.start()

    def sent(copy, local):
        if not local:
            copy.wait_send()

    def arrived(copy, local):
        copy.wait() if local else copy.wait_recv()


    def ring_step(step):
        for core in (c, 1 - c):
            for half in range(2):
                ring_copy(half, core, step, step - 1).wait_recv()

                @pl.when(step < steps)
                def _():
                    ring_copy(half, core, step, step).start()

        twin_copy(step, c).start()

    loop(1, 4, ring_step)
    known.start_flat()
    loop(4, 7, ring_step)
    known.relay()
    loop(7, steps + 1, ring_step)
    loop(1, CHIPS // 2 + c, lambda step: twin_copy(step, 1 - c).wait_recv())

    for half in range(2):
        move_out(half, start)
    everything = gathered[...].reshape(2, NB, K * NB)
    image = inner_product(trail[0], everything[0]) + inner_product(trail[1], everything[1])
    partial[...] = image.reshape(PROWS, 16, K * NB)

    def sum_copy(step, source):
        target = lax.rem(p + step, PROWS)
        return remote(partial.at[target], pieces.at[source], sum_send.at[step], sum_recv.at[source], target, q)

    loop(1, PROWS, lambda index: sum_copy(index, p).start())
    pieces[pl.ds(p, 1)] = partial[pl.ds(p, 1)]

    loop(0, NTOP, known.share)
    loop(0, NTOP, known.finish)
    for half in range(2):
        here_or_there(
            adjoint.at[0], moved.at[half], moved_send.at[0], moved_recv.at[half], home_row, 2 * p + half, arrived
        )

    loop(1, PROWS, lambda step: sum_copy(step, lax.rem(p + step, PROWS)).wait_recv())
    total = pieces[0]
    for source in range(1, PROWS):
        total = total + pieces[source]
    residual = moved[...].reshape(16, K * NB) - 2.0 * total

    def block(slot):
        return known_out[slot].reshape(NB, NB)

    parts = [residual[:, j * NB : (j + 1) * NB] for j in range(K)]
    for j in reversed(range(K)):
        parts[j] = matmul(parts[j], block(NBLK + j))
        for earlier in range(j):
            parts[earlier] = parts[earlier] - matmul(parts[j], block(block_slot(j, earlier)))
        solved[:, :, j * NB : (j + 1) * NB] = parts[j].reshape(2, 8, NB)
        for side in range(2):
            slices[2 * j + side] = parts[j][:, side * 128 : (side + 1) * 128]

    base, spot = (p // 8) * 8, lax.rem(p, 8)

    def slice_copy(step, source):
        target = lax.rem(spot + step, 8)
        return remote(slices.at[target], corner.at[source], slice_send.at[step], slice_recv.at[source], base + target, q)

    loop(1, 8, lambda step: slice_copy(step, spot).start())
    corner[pl.ds(spot, 1)] = slices[pl.ds(spot, 1)]

    def home_out(half, act):
        here_or_there(
            solved.at[half], home.at[home_half], home_send.at[half], home_recv.at[home_half],
            home_row, 2 * p + half, act,
        )

    loop(1, 8, lambda step: slice_copy(step, lax.rem(spot + step, 8)).wait_recv())
    tiles[...] = corner[...].reshape(128, 128).T.reshape(16, 8, 128)

    panel, upper = spot // 2, lax.rem(spot, 2)
    quarter = home_half * 2 + p // 8

    def tile_out(k, act):
        here_or_there(
            tiles.at[k], columns.at[panel, quarter], tile_send.at[k], tile_recv.at[panel, quarter],
            home_row, upper * 16 + k, act,
        )

    loop(0, 16, lambda k: tile_out(lax.rem(k + p, 16), start))

    def tile_in(index):
        j, part = index // 4, lax.rem(index, 4)
        source_row = lax.rem(part, 2) * 8 + 2 * j + home_half
        source_col = (part // 2) * PROWS + p
        here_or_there(
            tiles.at[0], columns.at[j, part], tile_send.at[0], tile_recv.at[j, part], source_row, source_col, arrived
        )

    loop(0, 16, tile_in)
    wide = jnp.concatenate([columns[:, part].reshape(32, 128) for part in range(4)], axis=1)
    gram = matmul(wide, gathered[...].reshape(2 * NB, K * NB))
    for j in range(K):
        for i in range(j + 1):
            terms[block_slot(j, i)] = gram[j * 8 : (j + 1) * 8, i * NB : (i + 1) * NB]

    def term_copy(target, source):
        return remote(terms.at[target], sums.at[source], term_send.at[target], term_recv.at[source], target, q)

    def each_term(act):
        def body(step):
            target = lax.rem(p + step, PROWS)

            @pl.when(target < NBLK)
            def _():
                act(term_copy(target, p))

        loop(1, PROWS, body)

    each_term(lambda copy: copy.start())

    loads[4].wait()

    @pl.when(p < NBLK)
    def _():
        own = lax.rem(p, NBLK)
        sums[pl.ds(p, 1)] = terms[pl.ds(own, 1)]

        def body(step):
            source = lax.rem(p + step, PROWS)
            term_copy(own, source).wait_recv()

        loop(1, PROWS, body)
        whole = sums[0]
        for source in range(1, PROWS):
            whole = whole + sums[source]
        open_out[pl.ds(p, 1), pl.ds(z, 1), pl.ds(c, 1)] = (top_adjoint[own] - whole)[None, None, None]

    opened.start_line()
    opened.start_flat()
    opened.relay()

    def share_column(j):
        for r in range(j, K):
            opened.share(block_slot(r, j))

    for j in reversed(range(K)):
        share_column(j)
    for half in range(2):
        home_out(half, start)
    for j in reversed(range(K)):
        for r in range(j, K):
            opened.finish(block_slot(r, j))
        top_column(j, known_out, open_out, full)
    top_out[...] = full[:, pl.ds(pl.multiple_of(q * 8, 8), 8), :]
    for half in range(2):
        here_or_there(
            solved.at[0], home.at[half], home_send.at[0], home_recv.at[half], z, half * PROWS + p, arrived
        )
    low_out[...] = home[...]

    for half in range(2):
        for core in range(2):
            loop(0, steps, lambda step: ring_copy(half, core, step, step).wait_send())
    own_copy(c).wait_send()
    loop(1, steps + 1, lambda step: twin_copy(step, c).wait_send())
    for half in range(2):
        move_out(half, sent)
        home_out(half, sent)
    loop(1, PROWS, lambda step: sum_copy(step, p).wait_send())
    loop(1, 8, lambda step: slice_copy(step, spot).wait_send())
    loop(0, 16, lambda k: tile_out(k, sent))
    each_term(lambda copy: copy.wait_send())
    known.drain()
    opened.drain()


def half_lower(square):
    row_ids = lax.broadcasted_iota(jnp.int32, (NB, NB), 0)
    col_ids = lax.broadcasted_iota(jnp.int32, (NB, NB), 1)
    return jnp.where(row_ids > col_ids, square, jnp.where(row_ids == col_ids, 0.5 * square, 0.0))


def lower(square):
    row_ids = lax.broadcasted_iota(jnp.int32, (NB, NB), 0)
    col_ids = lax.broadcasted_iota(jnp.int32, (NB, NB), 1)
    return jnp.where(row_ids >= col_ids, square, 0.0)


def top_column(j, known, opened, full):
    def factor(r, j):
        return known[block_slot(r, j)].reshape(NB, NB)

    def grad(r, j):
        return full[block_slot(r, j)]

    inverse = known[NBLK + j].reshape(NB, NB)
    for r in range(j + 1, K):
        rest = opened[block_slot(r, j)].reshape(NB, NB) - 2.0 * matmul(grad(r, r), factor(r, j))
        for middle in range(j + 1, r):
            rest = rest - matmul(grad(r, middle), factor(middle, j))
        for beyond in range(r + 1, K):
            rest = rest - inner_product(grad(beyond, r), factor(beyond, j))
        full[block_slot(r, j)] = matmul(rest, inverse)
    adj = opened[block_slot(j, j)].reshape(NB, NB)
    for r in range(j + 1, K):
        adj = adj - inner_product(grad(r, j), factor(r, j))
    inner = half_lower(inner_product(lower(factor(j, j)), lower(adj)))
    spread = inner_product(inverse, matmul(inner, inverse))
    full[block_slot(j, j)] = 0.5 * (spread + spread.T)


def per_device(adjoint_trail, factor_low, adjoint_low, factor_top, adjoint_top, diag_inverse):
    dma = pltpu.SemaphoreType.DMA
    vmem = pl.BlockSpec(memory_space=pltpu.VMEM)
    wide = K * NB
    low_grad, grad_top = pl.pallas_call(
        exchange_kernel,
        out_shape=[
            jax.ShapeDtypeStruct((2, 8, wide), F32),
            jax.ShapeDtypeStruct((NBLK, 8, NB), F32),
        ],
        in_specs=[vmem] + [pl.BlockSpec(memory_space=pltpu.MemorySpace.HBM)] * 5,
        out_specs=[vmem] * 2,
        scratch_shapes=[
            pltpu.VMEM((2, 8, K, NB), F32),
            pltpu.VMEM((2, 8, K, NB), F32),
            pltpu.VMEM((2, 8, wide), F32),
            pltpu.VMEM((NBLK, 8, NB), F32),
            pltpu.VMEM((NBLK, 8, NB), F32),
            pltpu.VMEM((K, 8, NB), F32),
            dma((5,)),
            pltpu.VMEM((NTOP, CHIPS, 2, 8, NB), F32),
            pltpu.VMEM((NBLK, CHIPS, 2, 8, NB), F32),
            pltpu.VMEM((NBLK, NB, NB), F32),
            pltpu.VMEM((2, PCOLS, 8, wide), F32),
            pltpu.VMEM((PROWS, 16, wide), F32),
            pltpu.VMEM((PROWS, 16, wide), F32),
            pltpu.VMEM((2, 8, wide), F32),
            pltpu.VMEM((2, 8, wide), F32),
            pltpu.VMEM((8, 16, 128), F32),
            pltpu.VMEM((8, 16, 128), F32),
            pltpu.VMEM((16, 8, 128), F32),
            pltpu.VMEM((4, 4, 8, 128), F32),
            pltpu.VMEM((PROWS, 8, NB), F32),
            pltpu.VMEM((NBLK, 8, NB), F32),
            pltpu.VMEM((2, 8, wide), F32),
            dma((2, 2, 8)), dma((2, 2, 8)), dma((9,)), dma((9,)), dma((2,)), dma((2,)),
            dma((PROWS,)), dma((PROWS,)), dma((2,)), dma((2,)), dma((8,)), dma((8,)),
            dma((16,)), dma((4, 4)), dma((NBLK,)), dma((PROWS,)),
            *spread_sems(NTOP),
            *spread_sems(NBLK),
        ],
        compiler_params=pltpu.CompilerParams(collective_id=0, has_side_effects=True, vmem_limit_bytes=40 * 1024 * 1024),
        name="exchange",
    )(
        adjoint_trail.reshape(2, NB, NB),
        factor_low.reshape(2, 8, K, NB),
        adjoint_low.reshape(2, 8, K, NB),
        factor_top,
        adjoint_top,
        diag_inverse,
    )
    return low_grad.reshape(factor_low.shape), grad_top


def solution(mesh):
    in_specs = (
        P(None, "prow", None, None, "pcol", None),
        P(None, "prow", "pcol", None, None, None),
        P(None, "prow", "pcol", None, None, None),
        P(None, "pcol", None),
        P(None, "pcol", None),
        P(None, "pcol", None),
    )
    out_specs = (P(None, "prow", "pcol", None, None, None), P(None, "pcol", None))
    return jax.shard_map(
        per_device, mesh=mesh, in_specs=in_specs, out_specs=out_specs, check_vma=False
    )
```

```python
import jax
import jax.numpy as jnp
from jax import lax
from jax.experimental import pallas as pl
from jax.experimental.pallas import tpu as pltpu
from jax.sharding import PartitionSpec as P

NB = 256
K = 4
NBLK = 10
NTOP = NBLK + K
PROWS = 16
PCOLS = 32
CHIPS = 16
SIDE = 4

MESH = pl.DeviceIdType.MESH
F32 = jnp.float32
BF16 = jnp.bfloat16


def split(array):
    high = array.astype(BF16)
    return high, (array - high.astype(F32)).astype(BF16)


def product(left, right, dims):
    (a, a_rest), (b, b_rest) = split(left), split(right)
    longer = jnp.concatenate([a, a, a_rest], axis=dims[0][0])
    taller = jnp.concatenate([b, b_rest, b], axis=dims[1][0])
    return lax.dot_general(longer, taller, (dims, ((), ())), preferred_element_type=F32)


def matmul(left, right):
    return product(left, right, ((1,), (0,)))


def inner_product(left, right):
    return product(left, right, ((0,), (0,)))


def block_slot(row_block, col_block):
    return row_block * (row_block + 1) // 2 + col_block


def loop(low, high, body):
    lax.fori_loop(low, high, lambda i, carry: (body(i), carry)[1], 0)


def remote(src, dst, send, recv, row, col):
    return pltpu.make_async_remote_copy(
        src_ref=src, dst_ref=dst, send_sem=send, recv_sem=recv, device_id=(row, col), device_id_type=MESH
    )


def far_first(index):
    rest = CHIPS - index
    odd = lax.rem(rest, 2)
    return (rest // 2 + 1) * odd + (CHIPS - rest // 2) * (1 - odd)


class Spread:
    def __init__(self, buf, count, sems, place):
        self.buf, self.count, self.place = buf, count, place
        self.line_send, self.line_recv, self.near_send, self.far_send, self.flat_recv, self.twin_send, self.twin_recv = sems

    def line_copy(self, step, origin):
        p, z, c = self.place
        tile = self.buf.at[p, origin, c]
        peer = lax.rem(z + step, CHIPS) * 2 + c
        return remote(tile, tile, self.line_send.at[step], self.line_recv.at[origin], p, peer)

    def peers(self, step):
        p, z, c = self.place
        x, y = p // SIDE, lax.rem(p, SIDE)
        along_x = lax.rem(x + step, SIDE) * SIDE + y
        along_y = x * SIDE + lax.rem(y + step, SIDE)
        return along_x * (1 - c) + along_y * c, along_y * (1 - c) + along_x * c

    def near_copy(self, step):
        p, z, c = self.place
        half = self.buf.at[p, :, c]
        return remote(half, half, self.near_send.at[step], self.flat_recv.at[p], self.peers(step)[0], z * 2 + c)

    def far_copy(self, block, origin, step):
        p, z, c = self.place
        half = self.buf.at[block, :, c]
        return remote(
            half, half, self.far_send.at[origin, step], self.flat_recv.at[block], self.peers(step)[1], z * 2 + c
        )

    def twin_copy(self, block, core):
        p, z, c = self.place
        half = self.buf.at[block, :, core]
        return remote(half, half, self.twin_send.at[block], self.twin_recv.at[block], p, z * 2 + 1 - c)

    def start_line(self):
        p, z, c = self.place

        @pl.when(p < self.count)
        def _():
            loop(1, CHIPS, lambda index: self.line_copy(far_first(index), z).start())

    def start_flat(self):
        p, z, c = self.place

        @pl.when(p < self.count)
        def _():
            loop(1, CHIPS, lambda step: self.line_copy(step, lax.rem(z + step, CHIPS)).wait_recv())

            for step in (1, 3, 2):
                self.near_copy(step).start()
            for step in (1, 3, 2):
                self.far_copy(p, 0, step).start()
            self.twin_copy(p, c).start()

    def relay(self):
        def body(origin):
            block = self.peers(origin)[0]

            @pl.when(block < self.count)
            def _():
                self.far_copy(block, origin, 1).wait_recv()
                for step in (1, 3, 2):
                    self.far_copy(block, origin, step).start()

        for origin in (1, 3, 2):
            body(origin)

    def share(self, block):
        p, z, c = self.place
        x, y = p // SIDE, lax.rem(p, SIDE)
        straight = (block // SIDE) * (1 - c) + lax.rem(block, SIDE) * c
        mine = x * (1 - c) + y * c
        cross = lax.rem(block, SIDE) * (1 - c) + (block // SIDE) * c
        level = y * (1 - c) + x * c

        @pl.when(block != p)
        def _():
            @pl.when((straight == mine) | (cross != level))
            def _():
                self.far_copy(block, 0, 1).wait_recv()

            self.twin_copy(block, c).start()

    def finish(self, block):
        p, z, c = self.place
        self.twin_copy(block, 1 - c).wait_recv()

    def drain(self):
        p, z, c = self.place

        @pl.when(p < self.count)
        def _():
            loop(1, CHIPS, lambda step: self.line_copy(step, z).wait_send())

            def body(step):
                self.near_copy(step).wait_send()
                self.far_copy(p, 0, step).wait_send()

            loop(1, SIDE, body)

        def relayed(origin):
            block = self.peers(origin)[0]

            @pl.when(block < self.count)
            def _():
                loop(1, SIDE, lambda step: self.far_copy(block, origin, step).wait_send())

        loop(1, SIDE, relayed)
        loop(0, self.count, lambda block: self.twin_copy(block, c).wait_send())


def spread_sems(count):
    dma = pltpu.SemaphoreType.DMA
    return [
        dma((CHIPS,)), dma((CHIPS,)), dma((SIDE,)), dma((SIDE, SIDE)), dma((PROWS,)), dma((count,)), dma((count,))
    ]


def exchange_kernel(
    trail, factor_in, adjoint_in, factor_top_in, adjoint_top_in, inverse_in, low_out, top_out,
    factor, adjoint_raw, adjoint, top_factor, top_adjoint, inverse, input_sems, known_out, open_out, full, gathered, partial, pieces, moved, solved, slices, corner, tiles, columns, sums, terms, home,
    ring_send, ring_recv, twin_send, twin_recv, moved_send, moved_recv, sum_send, sum_recv,
    home_send, home_recv, slice_send, slice_recv, tile_send, tile_recv, term_send, term_recv, *spreads
):
    p, q = lax.axis_index("prow"), lax.axis_index("pcol")
    z, c = q // 2, lax.rem(q, 2)
    place = (p, z, c)
    known = Spread(known_out, NTOP, spreads[:7], place)
    opened = Spread(open_out, NBLK, spreads[7:], place)

    home_row, home_half = lax.rem(q, PROWS), q // PROWS

    loads = [
        pltpu.make_async_copy(src, dst, input_sems.at[i])
        for i, (src, dst) in enumerate([
            (factor_in, factor), (factor_top_in, top_factor), (inverse_in, inverse),
            (adjoint_in, adjoint_raw), (adjoint_top_in, top_adjoint),
        ])
    ]
    for load in loads:
        load.start()

    barrier = pltpu.get_barrier_semaphore()

    def greet(row, col):
        @pl.when((row != p) | (col != q))
        def _():
            pl.semaphore_signal(barrier, inc=1, device_id=(row, col), device_id_type=MESH)

    loop(1, PROWS, lambda step: greet(lax.rem(p + step, PROWS), q))
    loop(1, PCOLS, lambda step: greet(p, lax.rem(q + step, PCOLS)))
    for half in range(2):
        greet(z, half * PROWS + p)
        greet(home_row, 2 * p + half)
    loads[0].wait()
    for j in range(K):
        gathered[:, pl.ds(q, 1), :, j * NB : (j + 1) * NB] = factor[:, :, j][:, None]
    own = 1 // (1 + (z - p) * (z - p) + (home_row - p) * (home_row - p))
    pl.semaphore_wait(barrier, PROWS + PCOLS + 2 - 2 * own)

    steps = CHIPS // 2 - c

    def origin_of(step, core):
        return lax.rem(z + (CHIPS - step) * (1 - core) + step * core, CHIPS)

    def ring_copy(half, core, step, slot):
        part = gathered.at[half, origin_of(step, c) * 2 + core]
        peer = lax.rem(z + 1 + (CHIPS - 2) * c, CHIPS)
        return remote(
            part, part, ring_send.at[half, core, slot], ring_recv.at[half, core, slot], p, peer * 2 + c
        )

    def own_copy(core):
        part = gathered.at[:, z * 2 + core]
        return remote(part, part, twin_send.at[0], twin_recv.at[0], p, z * 2 + 1 - c)

    def twin_copy(step, core):
        part = gathered.at[:, pl.ds(origin_of(step, core) * 2, 2)]
        return remote(part, part, twin_send.at[step], twin_recv.at[step], p, z * 2 + 1 - c)

    for half in range(2):
        ring_copy(half, c, 0, 0).start()
    own_copy(c).start()
    loads[1].wait()
    loads[2].wait()

    @pl.when(p < NBLK)
    def _():
        known_out[pl.ds(p, 1), pl.ds(z, 1), pl.ds(c, 1)] = top_factor[pl.ds(lax.rem(p, NBLK), 1)][:, None, None]

    @pl.when((p >= NBLK) & (p < NTOP))
    def _():
        known_out[pl.ds(p, 1), pl.ds(z, 1), pl.ds(c, 1)] = inverse[pl.ds(lax.rem(p + 2, K), 1)][:, None, None]

    known.start_line()
    own_copy(1 - c).wait_recv()
    for half in range(2):
        ring_copy(half, 1 - c, 0, 0).start()
    loads[3].wait()
    for j in range(K):
        adjoint[:, :, j * NB : (j + 1) * NB] = adjoint_raw[:, :, j]

    def here_or_there(src, dst, send, recv, row, col, act):
        own = (row == p) & (col == q)

        @pl.when(own)
        def _():
            act(pltpu.make_async_copy(src, dst, recv), True)

        @pl.when(jnp.logical_not(own))
        def _():
            act(remote(src, dst, send, recv, row, col), False)

    def move_out(half, act):
        here_or_there(
            adjoint.at[half], moved.at[c], moved_send.at[half], moved_recv.at[c], z, half * PROWS + p, act
        )

    def start(copy, local):
        copy.start()

    def sent(copy, local):
        if not local:
            copy.wait_send()

    def arrived(copy, local):
        copy.wait() if local else copy.wait_recv()


    def ring_step(step):
        for core in (c, 1 - c):
            for half in range(2):
                ring_copy(half, core, step, step - 1).wait_recv()

                @pl.when(step < steps)
                def _():
                    ring_copy(half, core, step, step).start()

        twin_copy(step, c).start()

    loop(1, 4, ring_step)
    known.start_flat()
    loop(4, 7, ring_step)
    known.relay()
    loop(7, steps + 1, ring_step)
    loop(1, CHIPS // 2 + c, lambda step: twin_copy(step, 1 - c).wait_recv())

    for half in range(2):
        move_out(half, start)
    everything = gathered[...].reshape(2, NB, K * NB)
    image = inner_product(trail[0], everything[0]) + inner_product(trail[1], everything[1])
    partial[...] = image.reshape(PROWS, 16, K * NB)

    def sum_copy(step, source):
        target = lax.rem(p + step, PROWS)
        return remote(partial.at[target], pieces.at[source], sum_send.at[step], sum_recv.at[source], target, q)

    loop(1, PROWS, lambda index: sum_copy(index, p).start())
    pieces[pl.ds(p, 1)] = partial[pl.ds(p, 1)]

    loop(0, NTOP, known.share)
    loop(0, NTOP, known.finish)
    for half in range(2):
        here_or_there(
            adjoint.at[0], moved.at[half], moved_send.at[0], moved_recv.at[half], home_row, 2 * p + half, arrived
        )

    loop(1, PROWS, lambda step: sum_copy(step, lax.rem(p + step, PROWS)).wait_recv())
    total = pieces[0]
    for source in range(1, PROWS):
        total = total + pieces[source]
    residual = moved[...].reshape(16, K * NB) - 2.0 * total

    def block(slot):
        return known_out[slot].reshape(NB, NB)

    parts = [residual[:, j * NB : (j + 1) * NB] for j in range(K)]
    for j in reversed(range(K)):
        parts[j] = matmul(parts[j], block(NBLK + j))
        for earlier in range(j):
            parts[earlier] = parts[earlier] - matmul(parts[j], block(block_slot(j, earlier)))
        solved[:, :, j * NB : (j + 1) * NB] = parts[j].reshape(2, 8, NB)
        for side in range(2):
            slices[2 * j + side] = parts[j][:, side * 128 : (side + 1) * 128]

    base, spot = (p // 8) * 8, lax.rem(p, 8)

    def slice_copy(step, source):
        target = lax.rem(spot + step, 8)
        return remote(slices.at[target], corner.at[source], slice_send.at[step], slice_recv.at[source], base + target, q)

    loop(1, 8, lambda step: slice_copy(step, spot).start())
    corner[pl.ds(spot, 1)] = slices[pl.ds(spot, 1)]

    def home_out(half, act):
        here_or_there(
            solved.at[half], home.at[home_half], home_send.at[half], home_recv.at[home_half],
            home_row, 2 * p + half, act,
        )

    loop(1, 8, lambda step: slice_copy(step, lax.rem(spot + step, 8)).wait_recv())
    tiles[...] = corner[...].reshape(128, 128).T.reshape(16, 8, 128)

    panel, upper = spot // 2, lax.rem(spot, 2)
    quarter = home_half * 2 + p // 8

    def tile_out(k, act):
        here_or_there(
            tiles.at[k], columns.at[panel, quarter], tile_send.at[k], tile_recv.at[panel, quarter],
            home_row, upper * 16 + k, act,
        )

    loop(0, 16, lambda k: tile_out(lax.rem(k + p, 16), start))

    def tile_in(index):
        j, part = index // 4, lax.rem(index, 4)
        source_row = lax.rem(part, 2) * 8 + 2 * j + home_half
        source_col = (part // 2) * PROWS + p
        here_or_there(
            tiles.at[0], columns.at[j, part], tile_send.at[0], tile_recv.at[j, part], source_row, source_col, arrived
        )

    loop(0, 16, tile_in)
    wide = jnp.concatenate([columns[:, part].reshape(32, 128) for part in range(4)], axis=1)
    gram = matmul(wide, gathered[...].reshape(2 * NB, K * NB))
    for j in range(K):
        for i in range(j + 1):
            terms[block_slot(j, i)] = gram[j * 8 : (j + 1) * 8, i * NB : (i + 1) * NB]

    def term_copy(target, source):
        return remote(terms.at[target], sums.at[source], term_send.at[target], term_recv.at[source], target, q)

    def each_term(act):
        def body(step):
            target = lax.rem(p + step, PROWS)

            @pl.when(target < NBLK)
            def _():
                act(term_copy(target, p))

        loop(1, PROWS, body)

    each_term(lambda copy: copy.start())

    loads[4].wait()

    @pl.when(p < NBLK)
    def _():
        own = lax.rem(p, NBLK)
        sums[pl.ds(p, 1)] = terms[pl.ds(own, 1)]

        def body(step):
            source = lax.rem(p + step, PROWS)
            term_copy(own, source).wait_recv()

        loop(1, PROWS, body)
        whole = sums[0]
        for source in range(1, PROWS):
            whole = whole + sums[source]
        open_out[pl.ds(p, 1), pl.ds(z, 1), pl.ds(c, 1)] = (top_adjoint[own] - whole)[None, None, None]

    opened.start_line()
    opened.start_flat()
    opened.relay()

    def share_column(j):
        for r in range(j, K):
            opened.share(block_slot(r, j))

    for j in reversed(range(K)):
        share_column(j)
    for half in range(2):
        home_out(half, start)
    for j in reversed(range(K)):
        for r in range(j, K):
            opened.finish(block_slot(r, j))
        top_column(j, known_out, open_out, full)
    top_out[...] = full[:, pl.ds(pl.multiple_of(q * 8, 8), 8), :]
    for half in range(2):
        here_or_there(
            solved.at[0], home.at[half], home_send.at[0], home_recv.at[half], z, half * PROWS + p, arrived
        )
    low_out[...] = home[...]

    for half in range(2):
        for core in range(2):
            loop(0, steps, lambda step: ring_copy(half, core, step, step).wait_send())
    own_copy(c).wait_send()
    loop(1, steps + 1, lambda step: twin_copy(step, c).wait_send())
    for half in range(2):
        move_out(half, sent)
        home_out(half, sent)
    loop(1, PROWS, lambda step: sum_copy(step, p).wait_send())
    loop(1, 8, lambda step: slice_copy(step, spot).wait_send())
    loop(0, 16, lambda k: tile_out(k, sent))
    each_term(lambda copy: copy.wait_send())
    known.drain()
    opened.drain()


def half_lower(square):
    row_ids = lax.broadcasted_iota(jnp.int32, (NB, NB), 0)
    col_ids = lax.broadcasted_iota(jnp.int32, (NB, NB), 1)
    return jnp.where(row_ids > col_ids, square, jnp.where(row_ids == col_ids, 0.5 * square, 0.0))


def lower(square):
    row_ids = lax.broadcasted_iota(jnp.int32, (NB, NB), 0)
    col_ids = lax.broadcasted_iota(jnp.int32, (NB, NB), 1)
    return jnp.where(row_ids >= col_ids, square, 0.0)


def top_column(j, known, opened, full):
    def factor(r, j):
        return known[block_slot(r, j)].reshape(NB, NB)

    def grad(r, j):
        return full[block_slot(r, j)]

    inverse = known[NBLK + j].reshape(NB, NB)
    for r in range(j + 1, K):
        rest = opened[block_slot(r, j)].reshape(NB, NB) - 2.0 * matmul(grad(r, r), factor(r, j))
        for middle in range(j + 1, r):
            rest = rest - matmul(grad(r, middle), factor(middle, j))
        for beyond in range(r + 1, K):
            rest = rest - inner_product(grad(beyond, r), factor(beyond, j))
        full[block_slot(r, j)] = matmul(rest, inverse)
    adj = opened[block_slot(j, j)].reshape(NB, NB)
    for r in range(j + 1, K):
        adj = adj - inner_product(grad(r, j), factor(r, j))
    inner = half_lower(inner_product(lower(factor(j, j)), lower(adj)))
    spread = inner_product(inverse, matmul(inner, inverse))
    full[block_slot(j, j)] = 0.5 * (spread + spread.T)


def per_device(adjoint_trail, factor_low, adjoint_low, factor_top, adjoint_top, diag_inverse):
    dma = pltpu.SemaphoreType.DMA
    vmem = pl.BlockSpec(memory_space=pltpu.VMEM)
    wide = K * NB
    low_grad, grad_top = pl.pallas_call(
        exchange_kernel,
        out_shape=[
            jax.ShapeDtypeStruct((2, 8, wide), F32),
            jax.ShapeDtypeStruct((NBLK, 8, NB), F32),
        ],
        in_specs=[vmem] + [pl.BlockSpec(memory_space=pltpu.MemorySpace.HBM)] * 5,
        out_specs=[vmem] * 2,
        scratch_shapes=[
            pltpu.VMEM((2, 8, K, NB), F32),
            pltpu.VMEM((2, 8, K, NB), F32),
            pltpu.VMEM((2, 8, wide), F32),
            pltpu.VMEM((NBLK, 8, NB), F32),
            pltpu.VMEM((NBLK, 8, NB), F32),
            pltpu.VMEM((K, 8, NB), F32),
            dma((5,)),
            pltpu.VMEM((NTOP, CHIPS, 2, 8, NB), F32),
            pltpu.VMEM((NBLK, CHIPS, 2, 8, NB), F32),
            pltpu.VMEM((NBLK, NB, NB), F32),
            pltpu.VMEM((2, PCOLS, 8, wide), F32),
            pltpu.VMEM((PROWS, 16, wide), F32),
            pltpu.VMEM((PROWS, 16, wide), F32),
            pltpu.VMEM((2, 8, wide), F32),
            pltpu.VMEM((2, 8, wide), F32),
            pltpu.VMEM((8, 16, 128), F32),
            pltpu.VMEM((8, 16, 128), F32),
            pltpu.VMEM((16, 8, 128), F32),
            pltpu.VMEM((4, 4, 8, 128), F32),
            pltpu.VMEM((PROWS, 8, NB), F32),
            pltpu.VMEM((NBLK, 8, NB), F32),
            pltpu.VMEM((2, 8, wide), F32),
            dma((2, 2, 8)), dma((2, 2, 8)), dma((9,)), dma((9,)), dma((2,)), dma((2,)),
            dma((PROWS,)), dma((PROWS,)), dma((2,)), dma((2,)), dma((8,)), dma((8,)),
            dma((16,)), dma((4, 4)), dma((NBLK,)), dma((PROWS,)),
            *spread_sems(NTOP),
            *spread_sems(NBLK),
        ],
        compiler_params=pltpu.CompilerParams(collective_id=0, has_side_effects=True, vmem_limit_bytes=40 * 1024 * 1024),
        name="exchange",
    )(
        adjoint_trail.reshape(2, NB, NB),
        factor_low.reshape(2, 8, K, NB),
        adjoint_low.reshape(2, 8, K, NB),
        factor_top,
        adjoint_top,
        diag_inverse,
    )
    return low_grad.reshape(factor_low.shape), grad_top


def solution(mesh):
    in_specs = (
        P(None, "prow", None, None, "pcol", None),
        P(None, "prow", "pcol", None, None, None),
        P(None, "prow", "pcol", None, None, None),
        P(None, "pcol", None),
        P(None, "pcol", None),
        P(None, "pcol", None),
    )
    out_specs = (P(None, "prow", "pcol", None, None, None), P(None, "pcol", None))
    return jax.shard_map(
        per_device, mesh=mesh, in_specs=in_specs, out_specs=out_specs, check_vma=False
    )
```
